128 devices in a mesh: region: 32 (over y, z, x_lo), col: 4 (over x_hi, core).
Axes of the slice: x: 4 (x_hi: 2, x_lo: 2; x = x_hi * 2 + x_lo), y: 4, z: 4, core: 2. Of those that a mesh axis runs over, the one named last changes fastest.
Arguments:
- basis_v: bfloat16 [196608, 512], P('region', 'col'), may hold values from -6 to 6
- basis_w: bfloat16 [196608, 512], P(('region', 'col')), may hold values from -0.0546875 to 0.0546875
- couplings: bfloat16 [1536, 48, 128, 128], P('region', 'col'), may hold values from -0.078125 to 0.078125
- coupling_cols: int32 [1536, 48], P('region', 'col'), may hold values from 0 to 1535, as said below
Outputs:
- reduced: float32 [512, 512], P(('region', 'col'))
The draws below stay inside these ranges and needn't reach their ends.
Inputs may be any that keep to these rules, and one draw needn't show every extreme that they name: `coupling_cols`: the 48 block columns of one block row are distinct and differ from its row number by at most 48; every block row takes the columns at distance 48 on both sides where they exist.
All inputs are finite; a program needn't handle non-finite values.
Results may differ from the reference program's by a relative error of at most 0.0003.
Values may be sent and summed in bfloat16 or wider, within the bound.
A program may use at most 192 MiB of HBM per device.

```python
import math
import jax
import jax.numpy as jnp
from jax import lax

BLOCK = 128
BASIS = 512
SLOTS = 48
REACH = 48
BLOCK_ROWS = 1536
STATES = 196608


def draw_coupling_cols(key, part):
    span = 2 * REACH + 1
    row_ids = jnp.arange(BLOCK_ROWS, dtype=jnp.int32)[:, None]
    offsets = jnp.arange(span, dtype=jnp.int32)[None, :] - REACH
    targets = row_ids + offsets
    valid = (targets >= 0) & (targets < BLOCK_ROWS)
    scores = jax.random.randint(key, (BLOCK_ROWS, span), 0, 2 ** 20, dtype=jnp.int32)
    scores = scores * span + jnp.arange(span, dtype=jnp.int32)[None, :]
    extreme = (offsets == REACH) | (offsets == -REACH)
    scores = jnp.where(extreme, scores + 2 ** 28, scores)
    scores = jnp.where(valid, scores, -1 - jnp.arange(span, dtype=jnp.int32)[None, :])
    unused, chosen = lax.top_k(scores, SLOTS)
    return jnp.take_along_axis(targets, chosen, axis=1).astype(jnp.int32)


def with_spikes(entries, rng, source, target, blocks, factor):
    owner, partner = [(jnp.arange(entries.shape[dim]) // (entries.shape[dim] // blocks)).reshape([-1 if axis == dim else 1 for axis in range(entries.ndim)]) for dim in (source, target)]
    chosen = jax.random.permutation(rng, blocks)[partner]
    strong = (owner == chosen) | (owner == (partner + blocks // 2) % blocks)
    return jnp.where(strong, factor * entries, entries)


def block_levels(stream_key, extent, split, low, largest):
    def one(axis_at, parts):
        heights = jax.random.uniform(jax.random.fold_in(jax.random.fold_in(stream_key, 6), axis_at), (parts,), jnp.float32, low / len(split), largest / len(split))
        return jnp.repeat(jnp.exp(heights), extent[axis_at] // parts).reshape((-1,) + (1,) * (len(extent) - axis_at - 1))

    gain = one(*split[0])
    for cut in split[1:]:
        gain = gain * one(*cut)
    return gain


def centred(key, extent, spread, bound, shards=(), kind=jnp.bfloat16):
    drawn = spread * jax.random.normal(key, extent, jnp.float32)
    if shards:
        drawn = drawn * block_levels(key, extent, shards, -0.22, 0.18)
    return jnp.clip(drawn, -bound, bound).astype(kind)


def gaussian_with(stream_key, dims, deviation, most, split, heavy, kind=jnp.bfloat16):
    result = deviation * jax.random.normal(stream_key, dims, jnp.float32)
    if split:
        result = result * block_levels(stream_key, dims, split, -0.22, 0.18)
    return jnp.clip(with_spikes(result, jax.random.fold_in(stream_key, 3), *heavy), -most, most).astype(kind)


def setup_inputs(seed: int = 0) -> dict:
    splits = jax.random.split(jax.random.key(seed), 5)
    basis_v = centred(splits[0], (STATES, BASIS), 1.0, 6.0, ((0, 32), (1, 4)))
    basis_w = gaussian_with(splits[1], (STATES, BASIS), STATES ** -0.5, 0.0546875, ((0, 128),), (0, 1, 128, 5.5))
    couplings = centred(splits[2], (BLOCK_ROWS, SLOTS, BLOCK, BLOCK), (SLOTS * BLOCK) ** -0.5, 0.078125, ((0, 32), (1, 4)))
    coupling_cols = draw_coupling_cols(jax.random.fold_in(splits[4], 71), 0)
    return dict(basis_v=basis_v, basis_w=basis_w, couplings=couplings, coupling_cols=coupling_cols)


def reference(basis_v, basis_w, couplings, coupling_cols):
    block_rows = coupling_cols.shape[0]
    block = couplings.shape[2]
    width = basis_v.shape[1]
    per_group = math.gcd(block_rows, 16)
    v_blocks = basis_v.reshape(block_rows, block, width)
    a_groups = couplings.reshape(block_rows // per_group, per_group, SLOTS, block, block)
    c_groups = coupling_cols.reshape(block_rows // per_group, per_group, SLOTS)
    w_groups = basis_w.reshape(block_rows // per_group, per_group * block, width)

    def advance(running, operands):
        blocks, columns, w_rows = operands
        picked = v_blocks[columns].astype(jnp.float32)
        coupled_image = jnp.einsum("gkrs,gksc->grc", blocks.astype(jnp.float32), picked, precision=lax.Precision.HIGHEST)
        coupled_image = coupled_image.reshape(per_group * block, width)
        running = running + jnp.einsum("rc,rd->cd", w_rows.astype(jnp.float32), coupled_image, precision=lax.Precision.HIGHEST)
        return running, None

    reduced, unused = lax.scan(advance, jnp.zeros((width, width), jnp.float32), (a_groups, c_groups, w_groups))
    return reduced
```

```python
import functools

import jax
import jax.numpy as jnp
from jax import lax
from jax.experimental import pallas as pl
from jax.experimental.pallas import tpu as pltpu
from jax.sharding import PartitionSpec as P

MESH = pl.DeviceIdType.MESH
CHUNKS = 8
HALF_CHUNKS = 2


def kernel(
    regions, cols_ref, a_hbm, v_hbm, w_hbm, o_ref,
    a, v, w, wr, hi, lo, acc, r0, t1, t2, rx, ry, u1, u2, r2x, r2y, fin, rf,
    loc, vs, vr, bs, br, ws, wrecv, qs_sem, qr_sem,
):
    nb, slots = a.shape[0], a.shape[1]
    n, half = CHUNKS, CHUNKS // 2
    cb = nb // n
    wb = w.shape[1]
    wh = wb // (2 * HALF_CHUNKS)
    pairs = regions // 2
    basis = acc.shape[-1]
    quarter = basis // 4

    r, q = lax.axis_index("region"), lax.axis_index("col")
    par, core, xh = r % 2, q % 2, q // 2
    k = r // 2
    q2 = (q + 2) % 4
    qs = q + 1 - 2 * core
    qs2 = (qs + 2) % 4
    partner = r + 1 - 2 * par
    dev_a = (partner, q)
    dev_b = (partner, q2)
    dev_d = (r, q2)
    dev_s = (r, qs)
    dev_z = ((r + 2 - 4 * par + regions) % regions, q)
    others = [(((k + j) % pairs) * 2 + par, q) for j in range(1, pairs)]
    here = nb
    near = 2 * nb * (1 - par)
    far = 2 * nb * par

    get_a = pltpu.make_async_copy(a_hbm, a, loc.at[0])
    get_v = pltpu.make_async_copy(v_hbm, v.at[q, pl.ds(here, nb)], loc.at[1])
    get_w = pltpu.make_async_copy(w_hbm, w.at[q], loc.at[2])
    get_v.start()
    get_w.start()

    barrier = pltpu.get_barrier_semaphore()
    greeted = [dev_a, dev_b, dev_d, dev_s] + others
    for dev in greeted:
        pl.semaphore_signal(barrier, inc=1, device_id=dev, device_id_type=MESH)
    pl.semaphore_wait(barrier, len(greeted))

    sent = []

    def send(src, dst, ssem, rsem, dev):
        copy = pltpu.make_async_remote_copy(
            src_ref=src, dst_ref=dst, send_sem=ssem, recv_sem=rsem,
            device_id=dev, device_id_type=MESH,
        )
        copy.start()
        sent.append(copy)

    def arrived(dst, rsem):
        pltpu.make_async_copy(dst, dst, rsem).wait()

    def piece(col, base, c):
        return v.at[col, pl.ds(base + c * cb, cb)]

    for t in range(n):
        c = t
        send(v_hbm.at[pl.ds(c * cb, cb)], piece(q, far, c), vs.at[0, c], vr.at[0, c], dev_a)
        c = (t + half) % n
        send(v_hbm.at[pl.ds(c * cb, cb)], piece(q, far, c), vs.at[1, c], vr.at[1, c], dev_b)
    send(v_hbm, v.at[q, pl.ds(here, nb)], bs.at[0, 0], br.at[0, 0], dev_s)
    send(w_hbm, w.at[q], ws.at[0], wrecv.at[0], dev_s)
    get_a.start()

    def to_sibling(slab, col, base, c):
        ref = piece(col, base, c)
        send(ref, ref, bs.at[slab, c], br.at[slab, c], dev_s)

    def take_a(c):
        arrived(piece(q, near, c), vr.at[0, c])
        src = piece(q, near, c)
        send(src, piece(q, far, c), vs.at[3, c], vr.at[3, c], dev_z)
        if c < half:
            send(src, piece(q, here, c), vs.at[2, c], vr.at[2, c], dev_b)
        to_sibling(1, q, near, c)

    def take_b(c):
        arrived(piece(q2, near, c), vr.at[1, c])
        src = piece(q2, near, c)
        send(src, piece(q2, far, c), vs.at[4, c], vr.at[4, c], dev_z)
        if c >= half:
            send(src, piece(q2, here, c), vs.at[2, c], vr.at[2, c], dev_a)
        to_sibling(2, q2, near, c)

    def take_d(c):
        arrived(piece(q2, here, c), vr.at[2, c])
        to_sibling(3, q2, here, c)

    def take_z(j):
        c = j // 2
        if j % 2 == 0:
            arrived(piece(q, far, c), vr.at[3, c])
            to_sibling(4, q, far, c)
        else:
            c = (c + half) % n
            arrived(piece(q2, far, c), vr.at[4, c])
            to_sibling(5, q2, far, c)

    for t in range(n):
        take_a(t)
        take_b((t + half) % n)

    for h in range(HALF_CHUNKS):
        send(w_hbm.at[pl.ds(h * wh, wh)], wr.at[0, h], ws.at[1 + h], wrecv.at[1 + h], dev_a)
        o = 1 + HALF_CHUNKS + h
        send(w_hbm.at[pl.ds(wb // 2 + h * wh, wh)], wr.at[1, h], ws.at[o], wrecv.at[o], dev_b)

    def relay_w(h):
        o = 1 + 2 * HALF_CHUNKS + h
        arrived(wr.at[0, h], wrecv.at[1 + h])
        send(wr.at[0, h], w.at[q, pl.ds(h * wh, wh)], ws.at[o], wrecv.at[o], dev_b)
        o = o + HALF_CHUNKS
        arrived(wr.at[1, h], wrecv.at[1 + HALF_CHUNKS + h])
        send(wr.at[1, h], w.at[q2, pl.ds(wb // 2 + h * wh, wh)], ws.at[o], wrecv.at[o], dev_a)

    zs = list(range(2 * n))
    for j in zs[: n // 2 + 2]:
        take_z(j)
    rest = zs[n // 2 + 2:]
    for t in range(half):
        take_d(t)
        take_d(t + half)
        if rest:
            take_z(rest.pop(0))
    for h in range(HALF_CHUNKS):
        for _ in range(len(rest) // (HALF_CHUNKS - h + 1)):
            take_z(rest.pop(0))
        relay_w(h)
    for j in rest:
        take_z(j)

    get_v.wait()
    get_a.wait()
    arrived(v.at[qs, pl.ds(here, nb)], br.at[0, 0])
    for c in range(n):
        arrived(piece(qs, near, c), br.at[1, c])
        arrived(piece(qs2, near, c), br.at[2, c])
        arrived(piece(qs2, here, c), br.at[3, c])
        arrived(piece(qs, far, c), br.at[4, c])
        arrived(piece(qs2, far, c), br.at[5, c])

    first = nb * r - nb

    def image_row(i, carry):
        ix = [jnp.clip(cols_ref[i, s] - first, 0, 3 * nb - 1) for s in range(slots)]
        lhs = jnp.concatenate([a[i, s] for s in range(slots)], axis=1)
        rhs = jnp.concatenate(
            [jnp.concatenate([v[c, at] for c in range(4)], axis=1) for at in ix], axis=0
        )
        total = jnp.dot(lhs, rhs, preferred_element_type=jnp.float32)
        upper = total.astype(jnp.bfloat16)
        hi[i] = upper
        lo[i] = (total - upper.astype(jnp.float32)).astype(jnp.bfloat16)
        return carry

    lax.fori_loop(0, nb, image_row, 0)

    for h in range(HALF_CHUNKS):
        for part in range(2):
            o = 1 + (2 + part) * HALF_CHUNKS + h
            ref = w.at[q2, pl.ds(part * (wb // 2) + h * wh, wh)]
            arrived(ref, wrecv.at[o])
            p = o + 2 * HALF_CHUNKS
            send(ref, ref, ws.at[p], wrecv.at[p], dev_s)
    get_w.wait()
    arrived(w.at[qs], wrecv.at[0])

    dims = (((0,), (0,)), ((), ()))

    def project(slab):
        rows = wb * w.shape[2]
        wv = w[slab].reshape(rows, basis)
        upper = hi[pl.ds(slab * wb, wb)].reshape(rows, basis)
        lower = lo[pl.ds(slab * wb, wb)].reshape(rows, basis)
        out = lax.dot_general(wv, upper, dims, preferred_element_type=jnp.float32)
        out += lax.dot_general(wv, lower, dims, preferred_element_type=jnp.float32)
        return out.reshape(acc.shape)

    acc[...] = project(q)
    acc[...] += project(qs)
    acc[...] += project(q2)
    for h in range(HALF_CHUNKS):
        for part in range(2):
            p = 1 + (4 + part) * HALF_CHUNKS + h
            arrived(w.at[qs2, pl.ds(part * (wb // 2) + h * wh, wh)], wrecv.at[p])
    acc[...] += project(qs2)

    mine = pl.multiple_of(core * (2 * quarter), 2 * quarter)
    theirs = pl.multiple_of((1 - core) * (2 * quarter), 2 * quarter)
    send(acc.at[:, :, :, pl.ds(theirs, 2 * quarter)], r0, qs_sem.at[0], qr_sem.at[0], dev_s)
    arrived(r0, qr_sem.at[0])
    t1[...] = acc[:, :, :, pl.ds(mine, quarter)] + r0[:, :, :, :quarter]
    t2[...] = acc[:, :, :, pl.ds(mine + quarter, quarter)] + r0[:, :, :, quarter:]

    xi = par * 2 + xh
    xis = [(1 - par) * 2 + xh, (1 - par) * 2 + (1 - xh), par * 2 + (1 - xh)]
    row = [dev_a, dev_b, dev_d]

    for e in range(3):
        send(t1.at[:, xis[e]], rx.at[e], qs_sem.at[1 + e], qr_sem.at[1 + e], row[e])
    for j in range(1, pairs):
        copy = pltpu.make_async_remote_copy(
            src_ref=t2.at[(k + j) % pairs], dst_ref=ry.at[j - 1],
            send_sem=qs_sem.at[4], recv_sem=qr_sem.at[4],
            device_id=others[j - 1], device_id_type=MESH,
        )
        copy.start()
    arrived(ry, qr_sem.at[4])
    u2[...] = t2[k] + sum(ry[j] for j in range(pairs - 1))
    for e in range(3):
        send(u2.at[xis[e]], r2x.at[e], qs_sem.at[5 + e], qr_sem.at[5 + e], row[e])
    for e in range(3):
        arrived(rx.at[e], qr_sem.at[1 + e])
    u1[...] = t1[:, xi] + (rx[0] + rx[1] + rx[2])
    for j in range(1, pairs):
        copy = pltpu.make_async_remote_copy(
            src_ref=u1.at[(k + j) % pairs], dst_ref=r2y.at[j - 1],
            send_sem=qs_sem.at[8], recv_sem=qr_sem.at[8],
            device_id=others[j - 1], device_id_type=MESH,
        )
        copy.start()
    for e in range(3):
        arrived(r2x.at[e], qr_sem.at[5 + e])
    second = u2[xi] + (r2x[0] + r2x[1] + r2x[2])
    arrived(r2y, qr_sem.at[8])
    fin[:, :quarter] = u1[k] + sum(r2y[j] for j in range(pairs - 1))
    fin[:, quarter:] = second
    send(fin, rf, qs_sem.at[9], qr_sem.at[9], dev_s)
    arrived(rf, qr_sem.at[9])
    own, other = fin[...], rf[...]
    left = jnp.where(core == 0, own, other)
    right = jnp.where(core == 0, other, own)
    rows = o_ref.shape[0]
    full = jnp.concatenate([left, right], axis=1)
    o_ref[...] = jnp.where(core == 0, full[:rows], full[rows:])

    pltpu.make_async_copy(ry, ry, qs_sem.at[4]).wait()
    pltpu.make_async_copy(r2y, r2y, qs_sem.at[8]).wait()
    for copy in sent:
        copy.wait_send()


def shards(regions, basis_v, basis_w, couplings, coupling_cols):
    nb, slots, block, _ = couplings.shape
    basis = basis_w.shape[1]
    wb = nb // 4
    wh = wb // (2 * HALF_CHUNKS)
    pairs = regions // 2
    group = basis // (4 * pairs)
    quarter = basis // 4
    bf16, f32 = jnp.bfloat16, jnp.float32
    dma = pltpu.SemaphoreType.DMA
    whole = pl.BlockSpec(memory_space=pl.ANY)
    return pl.pallas_call(
        functools.partial(kernel, regions),
        out_shape=jax.ShapeDtypeStruct((group // 2, basis), f32),
        in_specs=[pl.BlockSpec(memory_space=pltpu.SMEM), whole, whole, whole],
        out_specs=pl.BlockSpec(memory_space=pltpu.VMEM),
        scratch_shapes=[
            pltpu.VMEM((nb, slots, block, block), bf16),
            pltpu.VMEM((4, 3 * nb, block, quarter), bf16),
            pltpu.VMEM((4, wb, block, basis), bf16),
            pltpu.VMEM((2, HALF_CHUNKS, wh, block, basis), bf16),
            pltpu.VMEM((nb, block, basis), bf16),
            pltpu.VMEM((nb, block, basis), bf16),
            pltpu.VMEM((pairs, 4, group, basis), f32),
            pltpu.VMEM((pairs, 4, group, 2 * quarter), f32),
            pltpu.VMEM((pairs, 4, group, quarter), f32),
            pltpu.VMEM((pairs, 4, group, quarter), f32),
            pltpu.VMEM((3, pairs, group, quarter), f32),
            pltpu.VMEM((pairs - 1, 4, group, quarter), f32),
            pltpu.VMEM((pairs, group, quarter), f32),
            pltpu.VMEM((4, group, quarter), f32),
            pltpu.VMEM((3, group, quarter), f32),
            pltpu.VMEM((pairs - 1, group, quarter), f32),
            pltpu.VMEM((group, 2 * quarter), f32),
            pltpu.VMEM((group, 2 * quarter), f32),
            dma((3,)),
            dma((5, CHUNKS)), dma((5, CHUNKS)),
            dma((6, CHUNKS)), dma((6, CHUNKS)),
            dma((1 + 6 * HALF_CHUNKS,)), dma((1 + 6 * HALF_CHUNKS,)),
            dma((10,)), dma((10,)),
        ],
        compiler_params=pltpu.CompilerParams(
            collective_id=0, has_side_effects=True, vmem_limit_bytes=67043328
        ),
        name="project",
    )(
        coupling_cols,
        couplings,
        basis_v.reshape(nb, block, quarter),
        basis_w.reshape(wb, block, basis),
    )


def solution(mesh):
    in_specs = (
        P("region", "col"),
        P(("region", "col"), None),
        P("region", "col", None, None),
        P("region", "col"),
    )
    out_specs = P(("region", "col"), None)
    body = functools.partial(shards, mesh.shape["region"])
    return jax.shard_map(body, mesh=mesh, in_specs=in_specs, out_specs=out_specs, check_vma=False)
```

```python
import functools

import jax
import jax.numpy as jnp
from jax import lax
from jax.experimental import pallas as pl
from jax.experimental.pallas import tpu as pltpu
from jax.sharding import PartitionSpec as P

MESH = pl.DeviceIdType.MESH
CHUNKS = 8
EARLY, MIDDLE = 5, 2
HALF_CHUNKS = 3


def kernel(
    regions, cols_ref, a_hbm, v_hbm, w_hbm, o_ref,
    a, v, y1, y2, w, wr, hi, lo, acc, r0, t1, t2, rx, ry, u1, u2, r2x, r2y, fin, rf,
    loc, vs, vr, bs, br, ws, wrecv, qs_sem, qr_sem,
):
    nb, slots = a.shape[0], a.shape[1]
    n, half = CHUNKS, CHUNKS // 2
    cb = nb // n
    wb = w.shape[1]
    wh = wb // (2 * HALF_CHUNKS)
    pairs = regions // 2
    basis = acc.shape[-1]
    quarter = basis // 4

    r, q = lax.axis_index("region"), lax.axis_index("col")
    par, core, xh = r % 2, q % 2, q // 2
    k = r // 2
    q2 = (q + 2) % 4
    qs = q + 1 - 2 * core
    qs2 = (qs + 2) % 4
    partner = r + 1 - 2 * par
    dev_a = (partner, q)
    dev_b = (partner, q2)
    dev_d = (r, q2)
    dev_s = (r, qs)
    dev_z = ((r + 2 - 4 * par + regions) % regions, q)
    others = [(((k + j) % pairs) * 2 + par, q) for j in range(1, pairs)]
    ahead = EARLY * (nb // CHUNKS)

    def here(odd):
        return odd * nb + (1 - odd) * ahead

    def near(odd):
        return (1 - odd) * (nb + ahead)


    get_a = pltpu.make_async_copy(a_hbm, a, loc.at[0])
    get_v = pltpu.make_async_copy(v_hbm, v.at[q, pl.ds(here(par), nb)], loc.at[1])
    get_w = pltpu.make_async_copy(w_hbm, w.at[q], loc.at[2])
    get_v.start()
    get_w.start()

    barrier = pltpu.get_barrier_semaphore()
    greeted = [dev_a, dev_b, dev_d, dev_s] + others
    for dev in greeted:
        pl.semaphore_signal(barrier, inc=1, device_id=dev, device_id_type=MESH)
    pl.semaphore_wait(barrier, len(greeted))

    sent = []

    def send(src, dst, ssem, rsem, dev):
        copy = pltpu.make_async_remote_copy(
            src_ref=src, dst_ref=dst, send_sem=ssem, recv_sem=rsem,
            device_id=dev, device_id_type=MESH,
        )
        copy.start()
        sent.append(copy)

    def arrived(dst, rsem):
        pltpu.make_async_copy(dst, dst, rsem).wait()

    def place(odd, c):
        return odd * (n - 1 - c) * cb + (1 - odd) * c * cb

    def piece_here(col, odd, c):
        return v.at[col, pl.ds(here(odd) + place(odd, c), cb)]

    def piece_near(col, odd, c):
        return v.at[col, pl.ds(near(odd) + place(1 - odd, c), cb)]

    def piece_far(col, c):
        if c < EARLY:
            return v.at[col, pl.ds(par * (2 * nb + c * cb) + (1 - par) * (EARLY - 1 - c) * cb, cb)]
        if c < EARLY + MIDDLE:
            e = c - EARLY
            return y1.at[col, pl.ds(par * e * cb + (1 - par) * (MIDDLE - 1 - e) * cb, cb)]
        e, late = c - EARLY - MIDDLE, n - EARLY - MIDDLE
        return y2.at[col, pl.ds(par * e * cb + (1 - par) * (late - 1 - e) * cb, cb)]

    for c in range(n):
        src = v_hbm.at[pl.ds(place(par, c), cb)]
        send(src, piece_near(q, 1 - par, c), vs.at[0, c], vr.at[0, c], dev_a)
        send(src, piece_near(q, 1 - par, c), vs.at[1, c], vr.at[1, c], dev_b)
    send(v_hbm, v.at[q, pl.ds(here(par), nb)], bs.at[0, 0], br.at[0, 0], dev_s)
    send(w_hbm, w.at[q], ws.at[0], wrecv.at[0], dev_s)
    get_a.start()

    def to_sibling(slab, ref, c):
        send(ref, ref, bs.at[slab, c], br.at[slab, c], dev_s)

    def take_near(c):
        ref = piece_near(q, par, c)
        arrived(ref, vr.at[0, c])
        send(ref, piece_far(q, c), vs.at[3, c], vr.at[3, c], dev_z)
        if c < half:
            send(ref, piece_here(q, 1 - par, c), vs.at[2, c], vr.at[2, c], dev_b)
        to_sibling(1, ref, c)
        ref = piece_near(q2, par, c)
        arrived(ref, vr.at[1, c])
        send(ref, piece_far(q2, c), vs.at[4, c], vr.at[4, c], dev_z)
        if c >= half:
            send(ref, piece_here(q2, 1 - par, c), vs.at[2, c], vr.at[2, c], dev_a)
        to_sibling(2, ref, c)

    def take_here(c):
        ref = piece_here(q2, par, c)
        arrived(ref, vr.at[2, c])
        to_sibling(3, ref, c)

    def take_far(c):
        for e, col in ((3, q), (4, q2)):
            ref = piece_far(col, c)
            arrived(ref, vr.at[e, c])
            to_sibling(e + 1, ref, c)

    for c in range(n):
        take_near(c)

    for h in range(HALF_CHUNKS):
        send(w_hbm.at[pl.ds(h * wh, wh)], wr.at[0, h], ws.at[1 + h], wrecv.at[1 + h], dev_a)
        o = 1 + HALF_CHUNKS + h
        send(w_hbm.at[pl.ds(wb // 2 + h * wh, wh)], wr.at[1, h], ws.at[o], wrecv.at[o], dev_b)

    def relay_w(h):
        o = 1 + 2 * HALF_CHUNKS + h
        arrived(wr.at[0, h], wrecv.at[1 + h])
        send(wr.at[0, h], w.at[q, pl.ds(h * wh, wh)], ws.at[o], wrecv.at[o], dev_b)
        o = o + HALF_CHUNKS
        arrived(wr.at[1, h], wrecv.at[1 + HALF_CHUNKS + h])
        send(wr.at[1, h], w.at[q2, pl.ds(wb // 2 + h * wh, wh)], ws.at[o], wrecv.at[o], dev_a)

    for c in range(half - 1):
        take_far(c)
    for c in range(half):
        take_here(c)
        take_here(c + half)
        if c >= half - 2:
            take_far(half - 1 + c - (half - 2))

    get_v.wait()
    get_a.wait()
    arrived(v.at[qs, pl.ds(here(par), nb)], br.at[0, 0])
    for c in range(n):
        arrived(piece_near(qs, par, c), br.at[1, c])
        arrived(piece_near(qs2, par, c), br.at[2, c])
        arrived(piece_here(qs2, par, c), br.at[3, c])

    def image_rows(c):
        start = place(1 - par, c)
        held = [v] + ([y1] if c >= EARLY else []) + ([y2] if c >= EARLY + MIDDLE else [])
        away = nb * (r - 1 + 2 * par)
        bases = [
            nb * r - par * nb - (1 - par) * ahead,
            away + par * ahead + (1 - par) * (n - EARLY - MIDDLE) * cb,
            away + par * (EARLY + MIDDLE) * cb,
        ]

        def chosen(col, at):
            out = held[0][col, jnp.clip(at - bases[0], 0, held[0].shape[1] - 1)]
            for e in range(1, len(held)):
                inside = (at >= bases[e]) & (at < bases[e] + held[e].shape[1])
                other = held[e][col, jnp.clip(at - bases[e], 0, held[e].shape[1] - 1)]
                out = jnp.where(inside, other, out)
            return out

        def image_row(t, carry):
            i = start + t
            lhs = jnp.concatenate([a[i, s] for s in range(slots)], axis=1)
            rhs = jnp.concatenate(
                [
                    jnp.concatenate([chosen(col, cols_ref[s, i]) for col in range(4)], axis=1)
                    for s in range(slots)
                ],
                axis=0,
            )
            total = jnp.dot(lhs, rhs, preferred_element_type=jnp.float32)
            upper = total.astype(jnp.bfloat16)
            hi[i] = upper
            lo[i] = (total - upper.astype(jnp.float32)).astype(jnp.bfloat16)
            return carry

        lax.fori_loop(0, cb, image_row, 0)

    def all_far(first, last):
        for c in range(first, last):
            arrived(piece_far(qs, c), br.at[4, c])
            arrived(piece_far(qs2, c), br.at[5, c])

    all_far(0, EARLY)
    image_rows(0)
    take_far(5)
    image_rows(1)
    relay_w(0)
    image_rows(2)
    image_rows(3)
    relay_w(1)
    image_rows(4)
    take_far(6)
    all_far(EARLY, EARLY + MIDDLE)
    image_rows(5)
    relay_w(2)
    image_rows(6)
    take_far(7)
    all_far(EARLY + MIDDLE, n)
    image_rows(7)

    dims = (((0,), (0,)), ((), ()))

    def project(slab, at, count):
        rows = count * w.shape[2]
        wv = w[slab, at:at + count].reshape(rows, basis)
        upper = hi[pl.ds(slab * wb + at, count)].reshape(rows, basis)
        lower = lo[pl.ds(slab * wb + at, count)].reshape(rows, basis)
        out = lax.dot_general(wv, upper, dims, preferred_element_type=jnp.float32)
        out += lax.dot_general(wv, lower, dims, preferred_element_type=jnp.float32)
        return out.reshape(acc.shape)

    get_w.wait()
    acc[...] = project(q, 0, wb)
    arrived(w.at[qs], wrecv.at[0])
    acc[...] += project(qs, 0, wb)
    for h in range(HALF_CHUNKS):
        for part in range(2):
            o = 1 + (2 + part) * HALF_CHUNKS + h
            ref = w.at[q2, pl.ds(part * (wb // 2) + h * wh, wh)]
            arrived(ref, wrecv.at[o])
            p = o + 2 * HALF_CHUNKS
            send(ref, ref, ws.at[p], wrecv.at[p], dev_s)
        for part in range(2):
            acc[...] += project(q2, part * (wb // 2) + h * wh, wh)
        for part in range(2):
            p = 1 + (4 + part) * HALF_CHUNKS + h
            arrived(w.at[qs2, pl.ds(part * (wb // 2) + h * wh, wh)], wrecv.at[p])
            acc[...] += project(qs2, part * (wb // 2) + h * wh, wh)

    mine = pl.multiple_of(core * (2 * quarter), 2 * quarter)
    theirs = pl.multiple_of((1 - core) * (2 * quarter), 2 * quarter)
    send(acc.at[:, :, :, pl.ds(theirs, 2 * quarter)], r0, qs_sem.at[0], qr_sem.at[0], dev_s)
    arrived(r0, qr_sem.at[0])
    t1[...] = acc[:, :, :, pl.ds(mine, quarter)] + r0[:, :, :, :quarter]
    t2[...] = acc[:, :, :, pl.ds(mine + quarter, quarter)] + r0[:, :, :, quarter:]

    xi = par * 2 + xh
    xis = [(1 - par) * 2 + xh, (1 - par) * 2 + (1 - xh), par * 2 + (1 - xh)]
    row = [dev_a, dev_b, dev_d]

    for e in range(3):
        send(t1.at[:, xis[e]], rx.at[e], qs_sem.at[1 + e], qr_sem.at[1 + e], row[e])
    for j in range(1, pairs):
        copy = pltpu.make_async_remote_copy(
            src_ref=t2.at[(k + j) % pairs], dst_ref=ry.at[j - 1],
            send_sem=qs_sem.at[4], recv_sem=qr_sem.at[4],
            device_id=others[j - 1], device_id_type=MESH,
        )
        copy.start()
    arrived(ry, qr_sem.at[4])
    u2[...] = t2[k] + sum(ry[j] for j in range(pairs - 1))
    for e in range(3):
        send(u2.at[xis[e]], r2x.at[e], qs_sem.at[5 + e], qr_sem.at[5 + e], row[e])
    for e in range(3):
        arrived(rx.at[e], qr_sem.at[1 + e])
    u1[...] = t1[:, xi] + (rx[0] + rx[1] + rx[2])
    for j in range(1, pairs):
        copy = pltpu.make_async_remote_copy(
            src_ref=u1.at[(k + j) % pairs], dst_ref=r2y.at[j - 1],
            send_sem=qs_sem.at[8], recv_sem=qr_sem.at[8],
            device_id=others[j - 1], device_id_type=MESH,
        )
        copy.start()
    for e in range(3):
        arrived(r2x.at[e], qr_sem.at[5 + e])
    second = u2[xi] + (r2x[0] + r2x[1] + r2x[2])
    arrived(r2y, qr_sem.at[8])
    fin[:, :quarter] = u1[k] + sum(r2y[j] for j in range(pairs - 1))
    fin[:, quarter:] = second
    send(fin, rf, qs_sem.at[9], qr_sem.at[9], dev_s)
    arrived(rf, qr_sem.at[9])
    own, other = fin[...], rf[...]
    left = jnp.where(core == 0, own, other)
    right = jnp.where(core == 0, other, own)
    rows = o_ref.shape[0]
    full = jnp.concatenate([left, right], axis=1)
    o_ref[...] = jnp.where(core == 0, full[:rows], full[rows:])

    pltpu.make_async_copy(ry, ry, qs_sem.at[4]).wait()
    pltpu.make_async_copy(r2y, r2y, qs_sem.at[8]).wait()
    for copy in sent:
        copy.wait_send()


def shards(regions, basis_v, basis_w, couplings, coupling_cols):
    nb, slots, block, _ = couplings.shape
    basis = basis_w.shape[1]
    cb = nb // CHUNKS
    wb = nb // 4
    wh = wb // (2 * HALF_CHUNKS)
    pairs = regions // 2
    group = basis // (4 * pairs)
    quarter = basis // 4
    bf16, f32 = jnp.bfloat16, jnp.float32
    dma = pltpu.SemaphoreType.DMA
    whole = pl.BlockSpec(memory_space=pl.ANY)
    return pl.pallas_call(
        functools.partial(kernel, regions),
        out_shape=jax.ShapeDtypeStruct((group // 2, basis), f32),
        in_specs=[pl.BlockSpec(memory_space=pltpu.SMEM), whole, whole, whole],
        out_specs=pl.BlockSpec(memory_space=pltpu.VMEM),
        scratch_shapes=[
            pltpu.VMEM((nb, slots, block, block), bf16),
            pltpu.VMEM((4, 2 * nb + EARLY * cb, block, quarter), bf16),
            pltpu.VMEM((4, MIDDLE * cb, block, quarter), bf16),
            pltpu.VMEM((4, (CHUNKS - EARLY - MIDDLE) * cb, block, quarter), bf16),
            pltpu.VMEM((4, wb, block, basis), bf16),
            pltpu.VMEM((2, HALF_CHUNKS, wh, block, basis), bf16),
            pltpu.VMEM((nb, block, basis), bf16),
            pltpu.VMEM((nb, block, basis), bf16),
            pltpu.VMEM((pairs, 4, group, basis), f32),
            pltpu.VMEM((pairs, 4, group, 2 * quarter), f32),
            pltpu.VMEM((pairs, 4, group, quarter), f32),
            pltpu.VMEM((pairs, 4, group, quarter), f32),
            pltpu.VMEM((3, pairs, group, quarter), f32),
            pltpu.VMEM((pairs - 1, 4, group, quarter), f32),
            pltpu.VMEM((pairs, group, quarter), f32),
            pltpu.VMEM((4, group, quarter), f32),
            pltpu.VMEM((3, group, quarter), f32),
            pltpu.VMEM((pairs - 1, group, quarter), f32),
            pltpu.VMEM((group, 2 * quarter), f32),
            pltpu.VMEM((group, 2 * quarter), f32),
            dma((3,)),
            dma((5, CHUNKS)), dma((5, CHUNKS)),
            dma((6, CHUNKS)), dma((6, CHUNKS)),
            dma((1 + 6 * HALF_CHUNKS,)), dma((1 + 6 * HALF_CHUNKS,)),
            dma((10,)), dma((10,)),
        ],
        compiler_params=pltpu.CompilerParams(
            collective_id=0, has_side_effects=True, vmem_limit_bytes=67043328
        ),
        name="project",
    )(
        coupling_cols.T,
        couplings,
        basis_v.reshape(nb, block, quarter),
        basis_w.reshape(wb, block, basis),
    )


def solution(mesh):
    in_specs = (
        P("region", "col"),
        P(("region", "col"), None),
        P("region", "col", None, None),
        P("region", "col"),
    )
    out_specs = P(("region", "col"), None)
    body = functools.partial(shards, mesh.shape["region"])
    return jax.shard_map(body, mesh=mesh, in_specs=in_specs, out_specs=out_specs, check_vma=False)
```

```python
import functools

import jax
import jax.numpy as jnp
from jax import lax
from jax.experimental import pallas as pl
from jax.experimental.pallas import tpu as pltpu
from jax.sharding import PartitionSpec as P

MESH = pl.DeviceIdType.MESH
CHUNKS = 8
EARLY, MIDDLE = 5, 2
HALF_CHUNKS = 3


def kernel(
    regions, cols_ref, a_hbm, v_hbm, w_hbm, o_ref,
    a, v, y1, y2, w, wr, hi, lo, acc, r0, t1, t2, rx, ry, u1, u2, r2x, r2y, fin, rf,
    loc, vs, vr, bs, br, ws, wrecv, qs_sem, qr_sem,
):
    nb, slots = a.shape[0], a.shape[1]
    n, half = CHUNKS, CHUNKS // 2
    cb = nb // n
    wb = w.shape[1]
    wh = wb // (2 * HALF_CHUNKS)
    pairs = regions // 2
    basis = acc.shape[-1]
    quarter = basis // 4

    r, q = lax.axis_index("region"), lax.axis_index("col")
    par, core, xh = r % 2, q % 2, q // 2
    k = r // 2
    q2 = (q + 2) % 4
    qs = q + 1 - 2 * core
    qs2 = (qs + 2) % 4
    partner = r + 1 - 2 * par
    dev_a = (partner, q)
    dev_b = (partner, q2)
    dev_d = (r, q2)
    dev_s = (r, qs)
    dev_z = ((r + 2 - 4 * par + regions) % regions, q)
    others = [(((k + j) % pairs) * 2 + par, q) for j in range(1, pairs)]
    ahead = EARLY * (nb // CHUNKS)

    def here(odd):
        return odd * nb + (1 - odd) * ahead

    def near(odd):
        return (1 - odd) * (nb + ahead)


    get_a = pltpu.make_async_copy(a_hbm, a, loc.at[0])
    get_v = pltpu.make_async_copy(v_hbm, v.at[q, pl.ds(here(par), nb)], loc.at[1])
    get_w = pltpu.make_async_copy(w_hbm, w.at[q], loc.at[2])
    get_v.start()
    get_w.start()

    barrier = pltpu.get_barrier_semaphore()
    greeted = [dev_a, dev_b, dev_d, dev_s] + others
    for dev in greeted:
        pl.semaphore_signal(barrier, inc=1, device_id=dev, device_id_type=MESH)
    pl.semaphore_wait(barrier, len(greeted))

    sent = []

    def send(src, dst, ssem, rsem, dev):
        copy = pltpu.make_async_remote_copy(
            src_ref=src, dst_ref=dst, send_sem=ssem, recv_sem=rsem,
            device_id=dev, device_id_type=MESH,
        )
        copy.start()
        sent.append(copy)

    def arrived(dst, rsem):
        pltpu.make_async_copy(dst, dst, rsem).wait()

    def place(odd, c):
        return odd * (n - 1 - c) * cb + (1 - odd) * c * cb

    def piece_here(col, odd, c):
        return v.at[col, pl.ds(here(odd) + place(odd, c), cb)]

    def piece_near(col, odd, c):
        return v.at[col, pl.ds(near(odd) + place(1 - odd, c), cb)]

    def piece_far(col, c):
        if c < EARLY:
            return v.at[col, pl.ds(par * (2 * nb + c * cb) + (1 - par) * (EARLY - 1 - c) * cb, cb)]
        if c < EARLY + MIDDLE:
            e = c - EARLY
            return y1.at[col, pl.ds(par * e * cb + (1 - par) * (MIDDLE - 1 - e) * cb, cb)]
        e, late = c - EARLY - MIDDLE, n - EARLY - MIDDLE
        return y2.at[col, pl.ds(par * e * cb + (1 - par) * (late - 1 - e) * cb, cb)]

    for c in range(n):
        src = v_hbm.at[pl.ds(place(par, c), cb)]
        send(src, piece_near(q, 1 - par, c), vs.at[0, c], vr.at[0, c], dev_a)
        send(src, piece_near(q, 1 - par, c), vs.at[1, c], vr.at[1, c], dev_b)
    send(v_hbm, v.at[q, pl.ds(here(par), nb)], bs.at[0, 0], br.at[0, 0], dev_s)
    send(w_hbm, w.at[q], ws.at[0], wrecv.at[0], dev_s)
    get_a.start()

    def to_sibling(slab, ref, c):
        send(ref, ref, bs.at[slab, c], br.at[slab, c], dev_s)

    def take_near(c):
        ref = piece_near(q, par, c)
        arrived(ref, vr.at[0, c])
        send(ref, piece_far(q, c), vs.at[3, c], vr.at[3, c], dev_z)
        if c < half:
            send(ref, piece_here(q, 1 - par, c), vs.at[2, c], vr.at[2, c], dev_b)
        to_sibling(1, ref, c)
        ref = piece_near(q2, par, c)
        arrived(ref, vr.at[1, c])
        send(ref, piece_far(q2, c), vs.at[4, c], vr.at[4, c], dev_z)
        if c >= half:
            send(ref, piece_here(q2, 1 - par, c), vs.at[2, c], vr.at[2, c], dev_a)
        to_sibling(2, ref, c)

    def take_here(c):
        ref = piece_here(q2, par, c)
        arrived(ref, vr.at[2, c])
        to_sibling(3, ref, c)

    def take_far(c):
        for e, col in ((3, q), (4, q2)):
            ref = piece_far(col, c)
            arrived(ref, vr.at[e, c])
            to_sibling(e + 1, ref, c)

    for c in range(n):
        take_near(c)

    for h in range(HALF_CHUNKS):
        send(w_hbm.at[pl.ds(h * wh, wh)], wr.at[0, h], ws.at[1 + h], wrecv.at[1 + h], dev_a)
        o = 1 + HALF_CHUNKS + h
        send(w_hbm.at[pl.ds(wb // 2 + h * wh, wh)], wr.at[1, h], ws.at[o], wrecv.at[o], dev_b)

    def relay_w(h):
        o = 1 + 2 * HALF_CHUNKS + h
        arrived(wr.at[0, h], wrecv.at[1 + h])
        send(wr.at[0, h], w.at[q, pl.ds(h * wh, wh)], ws.at[o], wrecv.at[o], dev_b)
        o = o + HALF_CHUNKS
        arrived(wr.at[1, h], wrecv.at[1 + HALF_CHUNKS + h])
        send(wr.at[1, h], w.at[q2, pl.ds(wb // 2 + h * wh, wh)], ws.at[o], wrecv.at[o], dev_a)

    for c in range(half - 1):
        take_far(c)
    for c in range(half):
        take_here(c)
        take_here(c + half)
        if c >= half - 2:
            take_far(half - 1 + c - (half - 2))

    get_v.wait()
    get_a.wait()
    arrived(v.at[qs, pl.ds(here(par), nb)], br.at[0, 0])
    for c in range(n):
        arrived(piece_near(qs, par, c), br.at[1, c])
        arrived(piece_near(qs2, par, c), br.at[2, c])
        arrived(piece_here(qs2, par, c), br.at[3, c])

    def image_rows(c):
        start = place(1 - par, c)
        held = [v] + ([y1] if c >= EARLY else []) + ([y2] if c >= EARLY + MIDDLE else [])
        away = nb * (r - 1 + 2 * par)
        bases = [
            nb * r - par * nb - (1 - par) * ahead,
            away + par * ahead + (1 - par) * (n - EARLY - MIDDLE) * cb,
            away + par * (EARLY + MIDDLE) * cb,
        ]

        def chosen(col, at):
            out = held[0][col, jnp.clip(at - bases[0], 0, held[0].shape[1] - 1)]
            for e in range(1, len(held)):
                inside = (at >= bases[e]) & (at < bases[e] + held[e].shape[1])
                other = held[e][col, jnp.clip(at - bases[e], 0, held[e].shape[1] - 1)]
                out = jnp.where(inside, other, out)
            return out

        def image_row(t, carry):
            i = start + t
            lhs = jnp.concatenate([a[i, s] for s in range(slots)], axis=1)
            rhs = jnp.concatenate(
                [
                    jnp.concatenate([chosen(col, cols_ref[s, i]) for col in range(4)], axis=1)
                    for s in range(slots)
                ],
                axis=0,
            )
            total = jnp.dot(lhs, rhs, preferred_element_type=jnp.float32)
            upper = total.astype(jnp.bfloat16)
            hi[i] = upper
            lo[i] = (total - upper.astype(jnp.float32)).astype(jnp.bfloat16)
            return carry

        lax.fori_loop(0, cb, image_row, 0)

    def all_far(first, last):
        for c in range(first, last):
            arrived(piece_far(qs, c), br.at[4, c])
            arrived(piece_far(qs2, c), br.at[5, c])

    dims = (((0,), (0,)), ((), ()))

    def product(pieces):
        rows = sum(count for _, count, _ in pieces) * w.shape[2]
        wv = jnp.concatenate([wv for _, _, wv in pieces], axis=0).reshape(rows, basis)
        upper, lower = [
            jnp.concatenate([ref[pl.ds(at, count)] for at, count, _ in pieces], axis=0)
            .reshape(rows, basis)
            for ref in (hi, lo)
        ]
        out = lax.dot_general(wv, upper, dims, preferred_element_type=jnp.float32)
        out += lax.dot_general(wv, lower, dims, preferred_element_type=jnp.float32)
        return out.reshape(acc.shape)

    late = par * xh + (1 - par) * (1 - xh)

    def own_rows(m):
        at = (1 - par) * (n - 1 - m - late * half) * cb + par * (m + late * half) * cb
        slab = at // wb
        return at, cb, w[slab, pl.ds(at - slab * wb, cb)]

    def own_part(groups):
        return product([own_rows(m) for m in groups])

    all_far(0, EARLY)
    image_rows(0)
    take_far(5)
    image_rows(1)
    relay_w(0)
    image_rows(2)
    image_rows(3)
    relay_w(1)
    image_rows(4)
    take_far(6)
    all_far(EARLY, EARLY + MIDDLE)
    image_rows(5)
    relay_w(2)
    image_rows(6)
    get_w.wait()
    arrived(w.at[qs], wrecv.at[0])
    acc[...] = own_part([0, 1, 2])
    take_far(7)
    all_far(EARLY + MIDDLE, n)
    image_rows(7)
    acc[...] += own_part([3])

    def both(slab, h):
        ats = [part * (wb // 2) + h * wh for part in range(2)]
        return product([(slab * wb + at, wh, w[slab, at:at + wh]) for at in ats])

    for h in range(HALF_CHUNKS):
        for part in range(2):
            o = 1 + (2 + part) * HALF_CHUNKS + h
            ref = w.at[q2, pl.ds(part * (wb // 2) + h * wh, wh)]
            arrived(ref, wrecv.at[o])
            p = o + 2 * HALF_CHUNKS
            send(ref, ref, ws.at[p], wrecv.at[p], dev_s)
        acc[...] += both(q2, h)
        for part in range(2):
            p = 1 + (4 + part) * HALF_CHUNKS + h
            arrived(w.at[qs2, pl.ds(part * (wb // 2) + h * wh, wh)], wrecv.at[p])
        acc[...] += both(qs2, h)

    mine = pl.multiple_of(core * (2 * quarter), 2 * quarter)
    theirs = pl.multiple_of((1 - core) * (2 * quarter), 2 * quarter)
    for e in (1, 0):
        cut = acc.at[:, :, :, pl.ds(theirs + e * quarter, quarter)]
        send(cut, r0.at[e], qs_sem.at[e], qr_sem.at[e], dev_s)

    def scatter(src, dst, ssem, rsem):
        for j in range(1, pairs):
            pltpu.make_async_remote_copy(
                src_ref=src.at[(k + j) % pairs], dst_ref=dst.at[j - 1],
                send_sem=ssem, recv_sem=rsem,
                device_id=others[j - 1], device_id_type=MESH,
            ).start()

    xi = par * 2 + xh
    xis = [(1 - par) * 2 + xh, (1 - par) * 2 + (1 - xh), par * 2 + (1 - xh)]
    row = [dev_a, dev_b, dev_d]
    arrived(r0.at[1], qr_sem.at[1])
    t2[...] = acc[:, :, :, pl.ds(mine + quarter, quarter)] + r0[1]
    scatter(t2, ry, qs_sem.at[5], qr_sem.at[5])
    arrived(r0.at[0], qr_sem.at[0])
    t1[...] = acc[:, :, :, pl.ds(mine, quarter)] + r0[0]
    for e in range(3):
        send(t1.at[:, xis[e]], rx.at[e], qs_sem.at[2 + e], qr_sem.at[2 + e], row[e])
    for e in range(3):
        arrived(rx.at[e], qr_sem.at[2 + e])
    u1[...] = t1[:, xi] + (rx[0] + rx[1] + rx[2])
    scatter(u1, r2y, qs_sem.at[9], qr_sem.at[9])
    arrived(ry, qr_sem.at[5])
    u2[...] = t2[k] + sum(ry[j] for j in range(pairs - 1))
    for e in range(3):
        send(u2.at[xis[e]], r2x.at[e], qs_sem.at[6 + e], qr_sem.at[6 + e], row[e])
    for e in range(3):
        arrived(r2x.at[e], qr_sem.at[6 + e])
    second = u2[xi] + (r2x[0] + r2x[1] + r2x[2])
    arrived(r2y, qr_sem.at[9])
    fin[:, :quarter] = u1[k] + sum(r2y[j] for j in range(pairs - 1))
    fin[:, quarter:] = second
    send(fin, rf, qs_sem.at[10], qr_sem.at[10], dev_s)
    arrived(rf, qr_sem.at[10])
    own, other = fin[...], rf[...]
    left = jnp.where(core == 0, own, other)
    right = jnp.where(core == 0, other, own)
    rows = o_ref.shape[0]
    full = jnp.concatenate([left, right], axis=1)
    o_ref[...] = jnp.where(core == 0, full[:rows], full[rows:])

    arrived(ry, qs_sem.at[5])
    arrived(r2y, qs_sem.at[9])
    for copy in sent:
        copy.wait_send()


def shards(regions, basis_v, basis_w, couplings, coupling_cols):
    nb, slots, block, _ = couplings.shape
    basis = basis_w.shape[1]
    cb = nb // CHUNKS
    wb = nb // 4
    wh = wb // (2 * HALF_CHUNKS)
    pairs = regions // 2
    group = basis // (4 * pairs)
    quarter = basis // 4
    bf16, f32 = jnp.bfloat16, jnp.float32
    dma = pltpu.SemaphoreType.DMA
    whole = pl.BlockSpec(memory_space=pl.ANY)
    return pl.pallas_call(
        functools.partial(kernel, regions),
        out_shape=jax.ShapeDtypeStruct((group // 2, basis), f32),
        in_specs=[pl.BlockSpec(memory_space=pltpu.SMEM), whole, whole, whole],
        out_specs=pl.BlockSpec(memory_space=pltpu.VMEM),
        scratch_shapes=[
            pltpu.VMEM((nb, slots, block, block), bf16),
            pltpu.VMEM((4, 2 * nb + EARLY * cb, block, quarter), bf16),
            pltpu.VMEM((4, MIDDLE * cb, block, quarter), bf16),
            pltpu.VMEM((4, (CHUNKS - EARLY - MIDDLE) * cb, block, quarter), bf16),
            pltpu.VMEM((4, wb, block, basis), bf16),
            pltpu.VMEM((2, HALF_CHUNKS, wh, block, basis), bf16),
            pltpu.VMEM((nb, block, basis), bf16),
            pltpu.VMEM((nb, block, basis), bf16),
            pltpu.VMEM((pairs, 4, group, basis), f32),
            pltpu.VMEM((2, pairs, 4, group, quarter), f32),
            pltpu.VMEM((pairs, 4, group, quarter), f32),
            pltpu.VMEM((pairs, 4, group, quarter), f32),
            pltpu.VMEM((3, pairs, group, quarter), f32),
            pltpu.VMEM((pairs - 1, 4, group, quarter), f32),
            pltpu.VMEM((pairs, group, quarter), f32),
            pltpu.VMEM((4, group, quarter), f32),
            pltpu.VMEM((3, group, quarter), f32),
            pltpu.VMEM((pairs - 1, group, quarter), f32),
            pltpu.VMEM((group, 2 * quarter), f32),
            pltpu.VMEM((group, 2 * quarter), f32),
            dma((3,)),
            dma((5, CHUNKS)), dma((5, CHUNKS)),
            dma((6, CHUNKS)), dma((6, CHUNKS)),
            dma((1 + 6 * HALF_CHUNKS,)), dma((1 + 6 * HALF_CHUNKS,)),
            dma((11,)), dma((11,)),
        ],
        compiler_params=pltpu.CompilerParams(
            collective_id=0, has_side_effects=True, vmem_limit_bytes=67043328
        ),
        name="project",
    )(
        coupling_cols.T,
        couplings,
        basis_v.reshape(nb, block, quarter),
        basis_w.reshape(wb, block, basis),
    )


def solution(mesh):
    in_specs = (
        P("region", "col"),
        P(("region", "col"), None),
        P("region", "col", None, None),
        P("region", "col"),
    )
    out_specs = P(("region", "col"), None)
    body = functools.partial(shards, mesh.shape["region"])
    return jax.shard_map(body, mesh=mesh, in_specs=in_specs, out_specs=out_specs, check_vma=False)
```

```python
import functools

import jax
import jax.numpy as jnp
from jax import lax
from jax.experimental import pallas as pl
from jax.experimental.pallas import tpu as pltpu
from jax.sharding import PartitionSpec as P

MESH = pl.DeviceIdType.MESH
CHUNKS = 8
EARLY, MIDDLE = 5, 2
HALF_CHUNKS = 3


def kernel(
    regions, cols_ref, a_hbm, v_hbm, w_hbm, o_ref,
    a, v, y1, y2, w, wr, acc, r0, t1, t2, rx, ry, u1, u2, r2x, r2y, fin, rf,
    xs, loc, vs, vr, bs, br, ws, wrecv, xsend, xrecv, qs_sem, qr_sem,
):
    nb, slots = a.shape[0], a.shape[1]
    n, half = CHUNKS, CHUNKS // 2
    cb = nb // n
    wb = w.shape[1]
    wh = wb // (2 * HALF_CHUNKS)
    pairs = regions // 2
    basis = acc.shape[-1]
    quarter = basis // 4

    r, q = lax.axis_index("region"), lax.axis_index("col")
    par, core, xh = r % 2, q % 2, q // 2
    k = r // 2
    q2 = (q + 2) % 4
    qs = q + 1 - 2 * core
    qs2 = (qs + 2) % 4
    partner = r + 1 - 2 * par
    dev_a = (partner, q)
    dev_b = (partner, q2)
    dev_d = (r, q2)
    dev_s = (r, qs)
    dev_z = ((r + 2 - 4 * par + regions) % regions, q)
    others = [(((k + j) % pairs) * 2 + par, q) for j in range(1, pairs)]
    def near(odd):
        return 2 * nb * (1 - odd)

    get_a = pltpu.make_async_copy(a_hbm, a, loc.at[0])
    get_v = pltpu.make_async_copy(v_hbm, v.at[q, pl.ds(nb, nb)], loc.at[1])
    get_w = pltpu.make_async_copy(w_hbm, w.at[q], loc.at[2])
    get_v.start()
    get_w.start()

    barrier = pltpu.get_barrier_semaphore()
    greeted = [dev_a, dev_b, dev_d, dev_s] + others
    for dev in greeted:
        pl.semaphore_signal(barrier, inc=1, device_id=dev, device_id_type=MESH)
    pl.semaphore_wait(barrier, len(greeted))

    sent = []

    def send(src, dst, ssem, rsem, dev):
        copy = pltpu.make_async_remote_copy(
            src_ref=src, dst_ref=dst, send_sem=ssem, recv_sem=rsem,
            device_id=dev, device_id_type=MESH,
        )
        copy.start()
        sent.append(copy)

    def arrived(dst, rsem):
        pltpu.make_async_copy(dst, dst, rsem).wait()

    def place(odd, c):
        return odd * (n - 1 - c) * cb + (1 - odd) * c * cb

    def piece_here(col, odd, c):
        return v.at[col, pl.ds(nb + place(odd, c), cb)]

    def piece_near(col, odd, c):
        return v.at[col, pl.ds(near(odd) + place(1 - odd, c), cb)]

    def piece_far(col, c):
        if c < EARLY:
            return v.at[col, pl.ds(par * 2 * nb + place(1 - par, c), cb)]
        if c < EARLY + MIDDLE:
            e = c - EARLY
            return y1.at[col, pl.ds(par * e * cb + (1 - par) * (MIDDLE - 1 - e) * cb, cb)]
        e, late = c - EARLY - MIDDLE, n - EARLY - MIDDLE
        return y2.at[col, pl.ds(par * e * cb + (1 - par) * (late - 1 - e) * cb, cb)]

    for c in range(n):
        src = v_hbm.at[pl.ds(place(par, c), cb)]
        send(src, piece_near(q, 1 - par, c), vs.at[0, c], vr.at[0, c], dev_a)
        send(src, piece_near(q, 1 - par, c), vs.at[1, c], vr.at[1, c], dev_b)
    send(v_hbm, v.at[q, pl.ds(nb, nb)], bs.at[0, 0], br.at[0, 0], dev_s)
    send(w_hbm, w.at[q], ws.at[0], wrecv.at[0], dev_s)
    get_a.start()

    def to_sibling(slab, ref, c):
        send(ref, ref, bs.at[slab, c], br.at[slab, c], dev_s)

    def take_near(c):
        ref = piece_near(q, par, c)
        arrived(ref, vr.at[0, c])
        send(ref, piece_far(q, c), vs.at[3, c], vr.at[3, c], dev_z)
        if c < half:
            send(ref, piece_here(q, 1 - par, c), vs.at[2, c], vr.at[2, c], dev_b)
        to_sibling(1, ref, c)
        ref = piece_near(q2, par, c)
        arrived(ref, vr.at[1, c])
        send(ref, piece_far(q2, c), vs.at[4, c], vr.at[4, c], dev_z)
        if c >= half:
            send(ref, piece_here(q2, 1 - par, c), vs.at[2, c], vr.at[2, c], dev_a)
        to_sibling(2, ref, c)

    def take_here(c):
        ref = piece_here(q2, par, c)
        arrived(ref, vr.at[2, c])
        to_sibling(3, ref, c)

    def take_far(c):
        for e, col in ((3, q), (4, q2)):
            ref = piece_far(col, c)
            arrived(ref, vr.at[e, c])
            to_sibling(e + 1, ref, c)

    for c in range(n):
        take_near(c)

    for h in range(HALF_CHUNKS):
        send(w_hbm.at[pl.ds(h * wh, wh)], wr.at[0, h], ws.at[1 + h], wrecv.at[1 + h], dev_a)
        o = 1 + HALF_CHUNKS + h
        send(w_hbm.at[pl.ds(wb // 2 + h * wh, wh)], wr.at[1, h], ws.at[o], wrecv.at[o], dev_b)

    def relay_w(h):
        o = 1 + 2 * HALF_CHUNKS + h
        arrived(wr.at[0, h], wrecv.at[1 + h])
        send(wr.at[0, h], w.at[q, pl.ds(h * wh, wh)], ws.at[o], wrecv.at[o], dev_b)
        o = o + HALF_CHUNKS
        arrived(wr.at[1, h], wrecv.at[1 + HALF_CHUNKS + h])
        send(wr.at[1, h], w.at[q2, pl.ds(wb // 2 + h * wh, wh)], ws.at[o], wrecv.at[o], dev_a)

    for c in range(half - 1):
        take_far(c)
    for c in range(half):
        take_here(c)
        take_here(c + half)
        if c >= half - 2:
            take_far(half - 1 + c - (half - 2))

    get_v.wait()
    get_a.wait()
    arrived(v.at[qs, pl.ds(nb, nb)], br.at[0, 0])
    for c in range(n):
        arrived(piece_near(qs, par, c), br.at[1, c])
        arrived(piece_near(qs2, par, c), br.at[2, c])
        arrived(piece_here(qs2, par, c), br.at[3, c])

    def image_rows(c):
        start = place(1 - par, c)
        first = nb * r - nb

        def image_row(t, carry):
            i = start + t
            ix = [jnp.clip(cols_ref[s, i] - first, 0, 3 * nb - 1) for s in range(slots)]
            lhs = jnp.concatenate([a[i, s] for s in range(slots)], axis=1)
            rhs = jnp.concatenate(
                [jnp.concatenate([v[col, at] for col in range(4)], axis=1) for at in ix], axis=0
            )
            total = jnp.dot(lhs, rhs, preferred_element_type=jnp.float32)
            upper = total.astype(jnp.bfloat16)
            lower = (total - upper.astype(jnp.float32)).astype(jnp.bfloat16)
            for col in range(4):
                a[i, col] = upper[:, col * quarter:(col + 1) * quarter]
                a[i, 4 + col] = lower[:, col * quarter:(col + 1) * quarter]
            return carry

        lax.fori_loop(0, cb, image_row, 0)

    def all_far(first, last):
        for c in range(first, last):
            arrived(piece_far(qs, c), br.at[4, c])
            arrived(piece_far(qs2, c), br.at[5, c])

    dims = (((0,), (0,)), ((), ()))

    def image(at, count, first, cols=4):
        tiles = [a[pl.ds(at, count), first + e].reshape(count * a.shape[2], quarter) for e in range(cols)]
        return jnp.concatenate(tiles, axis=1)

    def product(pieces):
        rows = sum(count for _, count, _ in pieces) * w.shape[2]
        wv = jnp.concatenate([wv for _, _, wv in pieces], axis=0).reshape(rows, basis)
        upper, lower = [
            jnp.concatenate([image(at, count, e) for at, count, _ in pieces], axis=0)
            for e in (0, 4)
        ]
        out = lax.dot_general(wv, upper, dims, preferred_element_type=jnp.float32)
        out += lax.dot_general(wv, lower, dims, preferred_element_type=jnp.float32)
        return out.reshape(acc.shape)

    late = par * xh + (1 - par) * (1 - xh)

    def own_rows(m):
        at = (1 - par) * (n - 1 - m - late * half) * cb + par * (m + late * half) * cb
        slab = at // wb
        return at, cb, w[slab, pl.ds(at - slab * wb, cb)]

    def own_part(groups):
        return product([own_rows(m) for m in groups])

    at1 = par * (2 * nb + EARLY * cb) + (1 - par) * (n - EARLY - MIDDLE) * cb
    at2 = par * (2 * nb + (EARLY + MIDDLE) * cb)
    put1 = pltpu.make_async_copy(y1, v.at[:, pl.ds(at1, MIDDLE * cb)], loc.at[3])
    put2 = pltpu.make_async_copy(y2, v.at[:, pl.ds(at2, (n - EARLY - MIDDLE) * cb)], loc.at[4])

    all_far(0, EARLY)
    image_rows(0)
    take_far(5)
    image_rows(1)
    relay_w(0)
    image_rows(2)
    image_rows(3)
    relay_w(1)
    image_rows(4)
    take_far(6)
    all_far(EARLY, EARLY + MIDDLE)
    put1.start()
    get_w.wait()
    arrived(w.at[qs], wrecv.at[0])
    acc[...] = own_part([0])
    put1.wait()
    image_rows(5)
    relay_w(2)
    image_rows(6)
    take_far(7)
    all_far(EARLY + MIDDLE, n)
    put2.start()
    acc[...] += own_part([1, 2])
    put2.wait()
    image_rows(7)

    mine = pl.multiple_of(core * (2 * quarter), 2 * quarter)
    theirs = pl.multiple_of((1 - core) * (2 * quarter), 2 * quarter)
    last = HALF_CHUNKS - 1
    lasts = [(e, part) for e in range(2) for part in range(2)]

    def last_rows(slab, part):
        return slab * wb + part * (wb // 2) + last * wh

    for e, part in lasts:
        at = last_rows(2 * (1 - xh) + e, part)
        for f in range(2):
            cut = a.at[pl.ds(at, wh), pl.ds(4 * f + 2 * (1 - core), 2)]
            g = 4 * e + 2 * part + f
            send(cut, xs.at[e, part, f], xsend.at[g], xrecv.at[g], dev_s)
    acc[...] += own_part([3])

    def both(slab, h):
        ats = [part * (wb // 2) + h * wh for part in range(2)]
        return product([(slab * wb + at, wh, w[slab, at:at + wh]) for at in ats])

    def w_arrived(h):
        for part in range(2):
            o = 1 + (2 + part) * HALF_CHUNKS + h
            ref = w.at[q2, pl.ds(part * (wb // 2) + h * wh, wh)]
            arrived(ref, wrecv.at[o])
            p = o + 2 * HALF_CHUNKS
            send(ref, ref, ws.at[p], wrecv.at[p], dev_s)

    def w_forwarded(h):
        for part in range(2):
            p = 1 + (4 + part) * HALF_CHUNKS + h
            arrived(w.at[qs2, pl.ds(part * (wb // 2) + h * wh, wh)], wrecv.at[p])

    for h in range(last):
        w_arrived(h)
        acc[...] += both(q2, h)
        w_forwarded(h)
        acc[...] += both(qs2, h)

    for e in (1, 0):
        cut = acc.at[:, :, :, pl.ds(theirs + e * quarter, quarter)]
        send(cut, r0.at[e], qs_sem.at[e], qr_sem.at[e], dev_s)
    for e, part in lasts:
        for f in range(2):
            arrived(xs.at[e, part, f], xrecv.at[4 * e + 2 * part + f])
    arrived(r0.at[1], qr_sem.at[1])
    t2[...] = acc[:, :, :, pl.ds(mine + quarter, quarter)] + r0[1]
    arrived(r0.at[0], qr_sem.at[0])
    t1[...] = acc[:, :, :, pl.ds(mine, quarter)] + r0[0]

    def last_product(slab, e):
        rows = 2 * wh * w.shape[2]
        wv = jnp.concatenate(
            [w[slab, part * (wb // 2) + last * wh:part * (wb // 2) + (last + 1) * wh] for part in range(2)],
            axis=0,
        ).reshape(rows, basis)
        wv = jnp.concatenate([wv, wv], axis=0)
        out = None
        for f in range(2):
            img = jnp.concatenate(
                [image(last_rows(slab, part), wh, 4 * f + 2 * core, 2) for part in range(2)]
                + [
                    jnp.concatenate(
                        [xs[e, part, f, :, c].reshape(rows // 2, quarter) for c in range(2)], axis=1
                    )
                    for part in range(2)
                ],
                axis=0,
            )
            term = lax.dot_general(wv, img, dims, preferred_element_type=jnp.float32)
            out = term if out is None else out + term
        return out.reshape(t1.shape[:3] + (2 * quarter,))

    w_arrived(last)
    out = last_product(q2, core)
    t2[...] += out[:, :, :, quarter:]
    t1[...] += out[:, :, :, :quarter]
    w_forwarded(last)
    out = last_product(qs2, 1 - core)
    t2[...] += out[:, :, :, quarter:]
    t1[...] += out[:, :, :, :quarter]

    def scatter(src, dst, ssem, rsem):
        for j in range(1, pairs):
            pltpu.make_async_remote_copy(
                src_ref=src.at[(k + j) % pairs], dst_ref=dst.at[j - 1],
                send_sem=ssem, recv_sem=rsem,
                device_id=others[j - 1], device_id_type=MESH,
            ).start()

    xi = par * 2 + xh
    xis = [(1 - par) * 2 + xh, (1 - par) * 2 + (1 - xh), par * 2 + (1 - xh)]
    row = [dev_a, dev_b, dev_d]
    scatter(t2, ry, qs_sem.at[5], qr_sem.at[5])
    for e in range(3):
        send(t1.at[:, xis[e]], rx.at[e], qs_sem.at[2 + e], qr_sem.at[2 + e], row[e])
    for e in range(3):
        arrived(rx.at[e], qr_sem.at[2 + e])
    u1[...] = t1[:, xi] + (rx[0] + rx[1] + rx[2])
    scatter(u1, r2y, qs_sem.at[9], qr_sem.at[9])
    arrived(ry, qr_sem.at[5])
    u2[...] = t2[k] + sum(ry[j] for j in range(pairs - 1))
    for e in range(3):
        send(u2.at[xis[e]], r2x.at[e], qs_sem.at[6 + e], qr_sem.at[6 + e], row[e])
    for e in range(3):
        arrived(r2x.at[e], qr_sem.at[6 + e])
    second = u2[xi] + (r2x[0] + r2x[1] + r2x[2])
    arrived(r2y, qr_sem.at[9])
    fin[:, :quarter] = u1[k] + sum(r2y[j] for j in range(pairs - 1))
    fin[:, quarter:] = second
    send(fin, rf, qs_sem.at[10], qr_sem.at[10], dev_s)
    arrived(rf, qr_sem.at[10])
    own, other = fin[...], rf[...]
    left = jnp.where(core == 0, own, other)
    right = jnp.where(core == 0, other, own)
    rows = o_ref.shape[0]
    full = jnp.concatenate([left, right], axis=1)
    o_ref[...] = jnp.where(core == 0, full[:rows], full[rows:])

    arrived(ry, qs_sem.at[5])
    arrived(r2y, qs_sem.at[9])
    for copy in sent:
        copy.wait_send()


def shards(regions, basis_v, basis_w, couplings, coupling_cols):
    nb, slots, block, _ = couplings.shape
    basis = basis_w.shape[1]
    cb = nb // CHUNKS
    wb = nb // 4
    wh = wb // (2 * HALF_CHUNKS)
    pairs = regions // 2
    group = basis // (4 * pairs)
    quarter = basis // 4
    bf16, f32 = jnp.bfloat16, jnp.float32
    dma = pltpu.SemaphoreType.DMA
    whole = pl.BlockSpec(memory_space=pl.ANY)
    return pl.pallas_call(
        functools.partial(kernel, regions),
        out_shape=jax.ShapeDtypeStruct((group // 2, basis), f32),
        in_specs=[pl.BlockSpec(memory_space=pltpu.SMEM), whole, whole, whole],
        out_specs=pl.BlockSpec(memory_space=pltpu.VMEM),
        scratch_shapes=[
            pltpu.VMEM((nb, slots, block, block), bf16),
            pltpu.VMEM((4, 3 * nb, block, quarter), bf16),
            pltpu.VMEM((4, MIDDLE * cb, block, quarter), bf16),
            pltpu.VMEM((4, (CHUNKS - EARLY - MIDDLE) * cb, block, quarter), bf16),
            pltpu.VMEM((4, wb, block, basis), bf16),
            pltpu.VMEM((2, HALF_CHUNKS, wh, block, basis), bf16),
            pltpu.VMEM((pairs, 4, group, basis), f32),
            pltpu.VMEM((2, pairs, 4, group, quarter), f32),
            pltpu.VMEM((pairs, 4, group, quarter), f32),
            pltpu.VMEM((pairs, 4, group, quarter), f32),
            pltpu.VMEM((3, pairs, group, quarter), f32),
            pltpu.VMEM((pairs - 1, 4, group, quarter), f32),
            pltpu.VMEM((pairs, group, quarter), f32),
            pltpu.VMEM((4, group, quarter), f32),
            pltpu.VMEM((3, group, quarter), f32),
            pltpu.VMEM((pairs - 1, group, quarter), f32),
            pltpu.VMEM((group, 2 * quarter), f32),
            pltpu.VMEM((group, 2 * quarter), f32),
            pltpu.VMEM((2, 2, 2, wh, 2, block, quarter), bf16),
            dma((5,)),
            dma((5, CHUNKS)), dma((5, CHUNKS)),
            dma((6, CHUNKS)), dma((6, CHUNKS)),
            dma((1 + 6 * HALF_CHUNKS,)), dma((1 + 6 * HALF_CHUNKS,)),
            dma((8,)), dma((8,)),
            dma((11,)), dma((11,)),
        ],
        compiler_params=pltpu.CompilerParams(
            collective_id=0, has_side_effects=True, vmem_limit_bytes=67043328
        ),
        name="project",
    )(
        coupling_cols.T,
        couplings,
        basis_v.reshape(nb, block, quarter),
        basis_w.reshape(wb, block, basis),
    )


def solution(mesh):
    in_specs = (
        P("region", "col"),
        P(("region", "col"), None),
        P("region", "col", None, None),
        P("region", "col"),
    )
    out_specs = P(("region", "col"), None)
    body = functools.partial(shards, mesh.shape["region"])
    return jax.shard_map(body, mesh=mesh, in_specs=in_specs, out_specs=out_specs, check_vma=False)
```

```python
import functools

import jax
import jax.numpy as jnp
from jax import lax
from jax.experimental import pallas as pl
from jax.experimental.pallas import tpu as pltpu
from jax.sharding import PartitionSpec as P

MESH = pl.DeviceIdType.MESH
CHUNKS = 8
EARLY, MIDDLE = 5, 2
HALF_CHUNKS = 3


def kernel(
    regions, cols_ref, a_hbm, v_hbm, w_hbm, o_ref,
    a, v, y1, y2, w, wr, acc, r0, t1, t2, rx, ry, u1, u2, r2x, r2y, fin, rf,
    xs, loc, vs, vr, bs, br, ws, wrecv, xsend, xrecv, qs_sem, qr_sem,
):
    nb, slots = a.shape[0], a.shape[1]
    n, half = CHUNKS, CHUNKS // 2
    cb = nb // n
    wb = w.shape[1]
    wh = wb // (2 * HALF_CHUNKS)
    pairs = regions // 2
    basis = acc.shape[-1]
    quarter = basis // 4

    r, q = lax.axis_index("region"), lax.axis_index("col")
    par, core, xh = r % 2, q % 2, q // 2
    k = r // 2
    q2 = (q + 2) % 4
    qs = q + 1 - 2 * core
    qs2 = (qs + 2) % 4
    partner = r + 1 - 2 * par
    dev_a = (partner, q)
    dev_b = (partner, q2)
    dev_d = (r, q2)
    dev_s = (r, qs)
    dev_z = ((r + 2 - 4 * par + regions) % regions, q)
    others = [(((k + j) % pairs) * 2 + par, q) for j in range(1, pairs)]
    def near(odd):
        return 2 * nb * (1 - odd)

    get_a = pltpu.make_async_copy(a_hbm, a, loc.at[0])
    get_v = pltpu.make_async_copy(v_hbm, v.at[q, pl.ds(nb, nb)], loc.at[1])
    get_w = pltpu.make_async_copy(w_hbm, w.at[q], loc.at[2])
    get_v.start()
    get_w.start()

    barrier = pltpu.get_barrier_semaphore()
    greeted = [dev_a, dev_b, dev_d, dev_s] + others
    for dev in greeted:
        pl.semaphore_signal(barrier, inc=1, device_id=dev, device_id_type=MESH)
    pl.semaphore_wait(barrier, len(greeted))

    sent = []

    def send(src, dst, ssem, rsem, dev):
        copy = pltpu.make_async_remote_copy(
            src_ref=src, dst_ref=dst, send_sem=ssem, recv_sem=rsem,
            device_id=dev, device_id_type=MESH,
        )
        copy.start()
        sent.append(copy)

    def arrived(dst, rsem):
        pltpu.make_async_copy(dst, dst, rsem).wait()

    def place(odd, c):
        return odd * (n - 1 - c) * cb + (1 - odd) * c * cb

    def piece_here(col, odd, c):
        return v.at[col, pl.ds(nb + place(odd, c), cb)]

    def piece_near(col, odd, c):
        return v.at[col, pl.ds(near(odd) + place(1 - odd, c), cb)]

    def piece_far(col, c):
        if c < EARLY:
            return v.at[col, pl.ds(par * 2 * nb + place(1 - par, c), cb)]
        if c < EARLY + MIDDLE:
            e = c - EARLY
            return y1.at[col, pl.ds(par * e * cb + (1 - par) * (MIDDLE - 1 - e) * cb, cb)]
        e, late = c - EARLY - MIDDLE, n - EARLY - MIDDLE
        return y2.at[col, pl.ds(par * e * cb + (1 - par) * (late - 1 - e) * cb, cb)]

    for c in range(n):
        src = v_hbm.at[pl.ds(place(par, c), cb)]
        send(src, piece_near(q, 1 - par, c), vs.at[0, c], vr.at[0, c], dev_a)
        send(src, piece_near(q, 1 - par, c), vs.at[1, c], vr.at[1, c], dev_b)
    send(v_hbm, v.at[q, pl.ds(nb, nb)], bs.at[0, 0], br.at[0, 0], dev_s)
    send(w_hbm, w.at[q], ws.at[0], wrecv.at[0], dev_s)
    get_a.start()

    def to_sibling(slab, ref, c):
        send(ref, ref, bs.at[slab, c], br.at[slab, c], dev_s)

    def take_near(c):
        ref = piece_near(q, par, c)
        arrived(ref, vr.at[0, c])
        send(ref, piece_far(q, c), vs.at[3, c], vr.at[3, c], dev_z)
        if c < half:
            send(ref, piece_here(q, 1 - par, c), vs.at[2, c], vr.at[2, c], dev_b)
        to_sibling(1, ref, c)
        ref = piece_near(q2, par, c)
        arrived(ref, vr.at[1, c])
        send(ref, piece_far(q2, c), vs.at[4, c], vr.at[4, c], dev_z)
        if c >= half:
            send(ref, piece_here(q2, 1 - par, c), vs.at[2, c], vr.at[2, c], dev_a)
        to_sibling(2, ref, c)

    def take_here(c):
        ref = piece_here(q2, par, c)
        arrived(ref, vr.at[2, c])
        to_sibling(3, ref, c)

    def take_far(c):
        for e, col in ((3, q), (4, q2)):
            ref = piece_far(col, c)
            arrived(ref, vr.at[e, c])
            to_sibling(e + 1, ref, c)

    for c in range(n):
        take_near(c)

    for h in range(HALF_CHUNKS):
        send(w_hbm.at[pl.ds(h * wh, wh)], wr.at[0, h], ws.at[1 + h], wrecv.at[1 + h], dev_a)
        o = 1 + HALF_CHUNKS + h
        send(w_hbm.at[pl.ds(wb // 2 + h * wh, wh)], wr.at[1, h], ws.at[o], wrecv.at[o], dev_b)

    def relay_w(h):
        o = 1 + 2 * HALF_CHUNKS + h
        arrived(wr.at[0, h], wrecv.at[1 + h])
        send(wr.at[0, h], w.at[q, pl.ds(h * wh, wh)], ws.at[o], wrecv.at[o], dev_b)
        o = o + HALF_CHUNKS
        arrived(wr.at[1, h], wrecv.at[1 + HALF_CHUNKS + h])
        send(wr.at[1, h], w.at[q2, pl.ds(wb // 2 + h * wh, wh)], ws.at[o], wrecv.at[o], dev_a)

    for c in range(half - 1):
        take_far(c)
    for c in range(half):
        take_here(c)
        take_here(c + half)
        if c >= half - 2:
            take_far(half - 1 + c - (half - 2))

    get_v.wait()
    get_a.wait()
    arrived(v.at[qs, pl.ds(nb, nb)], br.at[0, 0])
    for c in range(n):
        arrived(piece_near(qs, par, c), br.at[1, c])
        arrived(piece_near(qs2, par, c), br.at[2, c])
        arrived(piece_here(qs2, par, c), br.at[3, c])

    def image_rows(c):
        start = place(1 - par, c)
        first = nb * r - nb

        def image_row(t, carry):
            i = start + t
            ix = [jnp.clip(cols_ref[s, i] - first, 0, 3 * nb - 1) for s in range(slots)]
            lhs = jnp.concatenate([a[i, s] for s in range(slots)], axis=1)
            rhs = jnp.concatenate(
                [jnp.concatenate([v[col, at] for col in range(4)], axis=1) for at in ix], axis=0
            )
            total = jnp.dot(lhs, rhs, preferred_element_type=jnp.float32)
            upper = total.astype(jnp.bfloat16)
            lower = (total - upper.astype(jnp.float32)).astype(jnp.bfloat16)
            for col in range(4):
                a[i, col] = upper[:, col * quarter:(col + 1) * quarter]
                a[i, 4 + col] = lower[:, col * quarter:(col + 1) * quarter]
            return carry

        lax.fori_loop(0, cb, image_row, 0)

    def all_far(first, last):
        for c in range(first, last):
            arrived(piece_far(qs, c), br.at[4, c])
            arrived(piece_far(qs2, c), br.at[5, c])

    dims = (((0,), (0,)), ((), ()))

    def image(at, count, first, cols=4):
        tiles = [a[pl.ds(at, count), first + e].reshape(count * a.shape[2], quarter) for e in range(cols)]
        return jnp.concatenate(tiles, axis=1)

    def product(pieces):
        rows = sum(count for _, count, _ in pieces) * w.shape[2]
        wv = jnp.concatenate([wv for _, _, wv in pieces], axis=0).reshape(rows, basis)
        upper, lower = [
            jnp.concatenate([image(at, count, e) for at, count, _ in pieces], axis=0)
            for e in (0, 4)
        ]
        out = lax.dot_general(wv, upper, dims, preferred_element_type=jnp.float32)
        out += lax.dot_general(wv, lower, dims, preferred_element_type=jnp.float32)
        return out.reshape(acc.shape)

    late = par * xh + (1 - par) * (1 - xh)

    def own_rows(m):
        at = (1 - par) * (n - 1 - m - late * half) * cb + par * (m + late * half) * cb
        slab = at // wb
        return at, cb, w[slab, pl.ds(at - slab * wb, cb)]

    def own_part(groups):
        return product([own_rows(m) for m in groups])

    at1 = par * (2 * nb + EARLY * cb) + (1 - par) * (n - EARLY - MIDDLE) * cb
    at2 = par * (2 * nb + (EARLY + MIDDLE) * cb)
    put1 = pltpu.make_async_copy(y1, v.at[:, pl.ds(at1, MIDDLE * cb)], loc.at[3])
    put2 = pltpu.make_async_copy(y2, v.at[:, pl.ds(at2, (n - EARLY - MIDDLE) * cb)], loc.at[4])

    def w_arrived(h):
        for part in range(2):
            o = 1 + (2 + part) * HALF_CHUNKS + h
            ref = w.at[q2, pl.ds(part * (wb // 2) + h * wh, wh)]
            arrived(ref, wrecv.at[o])
            p = o + 2 * HALF_CHUNKS
            send(ref, ref, ws.at[p], wrecv.at[p], dev_s)

    def w_forwarded(h):
        for part in range(2):
            p = 1 + (4 + part) * HALF_CHUNKS + h
            arrived(w.at[qs2, pl.ds(part * (wb // 2) + h * wh, wh)], wrecv.at[p])

    all_far(0, EARLY)
    image_rows(0)
    take_far(5)
    image_rows(1)
    relay_w(0)
    image_rows(2)
    image_rows(3)
    relay_w(1)
    image_rows(4)
    take_far(6)
    all_far(EARLY, EARLY + MIDDLE)
    put1.start()
    get_w.wait()
    arrived(w.at[qs], wrecv.at[0])
    acc[...] = own_part([0])
    put1.wait()
    image_rows(5)
    relay_w(2)
    image_rows(6)
    acc[...] += own_part([1, 2])
    take_far(7)
    all_far(EARLY + MIDDLE, n)
    put2.start()
    w_arrived(0)
    put2.wait()
    image_rows(7)

    mine = pl.multiple_of(core * (2 * quarter), 2 * quarter)
    theirs = pl.multiple_of((1 - core) * (2 * quarter), 2 * quarter)
    last = HALF_CHUNKS - 1
    lasts = [(e, part) for e in range(2) for part in range(2)]

    def last_rows(slab, part):
        return slab * wb + part * (wb // 2) + last * wh

    for e, part in lasts:
        at = last_rows(2 * (1 - xh) + e, part)
        for f in range(2):
            cut = a.at[pl.ds(at, wh), pl.ds(4 * f + 2 * (1 - core), 2)]
            g = 4 * e + 2 * part + f
            send(cut, xs.at[e, part, f], xsend.at[g], xrecv.at[g], dev_s)
    acc[...] += own_part([3])

    def both(slab, h):
        ats = [part * (wb // 2) + h * wh for part in range(2)]
        return product([(slab * wb + at, wh, w[slab, at:at + wh]) for at in ats])

    for h in range(1, last):
        w_arrived(h)
    for h in range(last):
        w_forwarded(h)
        acc[...] += both(q2, h) + both(qs2, h)

    for e in (1, 0):
        cut = acc.at[:, :, :, pl.ds(theirs + e * quarter, quarter)]
        send(cut, r0.at[e], qs_sem.at[e], qr_sem.at[e], dev_s)
    for e, part in lasts:
        for f in range(2):
            arrived(xs.at[e, part, f], xrecv.at[4 * e + 2 * part + f])
    arrived(r0.at[1], qr_sem.at[1])
    t2[...] = acc[:, :, :, pl.ds(mine + quarter, quarter)] + r0[1]
    arrived(r0.at[0], qr_sem.at[0])
    t1[...] = acc[:, :, :, pl.ds(mine, quarter)] + r0[0]

    def last_product(slab, e):
        rows = 2 * wh * w.shape[2]
        wv = jnp.concatenate(
            [w[slab, part * (wb // 2) + last * wh:part * (wb // 2) + (last + 1) * wh] for part in range(2)],
            axis=0,
        ).reshape(rows, basis)
        wv = jnp.concatenate([wv, wv], axis=0)
        out = None
        for f in range(2):
            img = jnp.concatenate(
                [image(last_rows(slab, part), wh, 4 * f + 2 * core, 2) for part in range(2)]
                + [
                    jnp.concatenate(
                        [xs[e, part, f, :, c].reshape(rows // 2, quarter) for c in range(2)], axis=1
                    )
                    for part in range(2)
                ],
                axis=0,
            )
            term = lax.dot_general(wv, img, dims, preferred_element_type=jnp.float32)
            out = term if out is None else out + term
        return out.reshape(t1.shape[:3] + (2 * quarter,))

    w_arrived(last)
    out = last_product(q2, core)
    t2[...] += out[:, :, :, quarter:]
    t1[...] += out[:, :, :, :quarter]
    w_forwarded(last)
    out = last_product(qs2, 1 - core)
    t2[...] += out[:, :, :, quarter:]
    t1[...] += out[:, :, :, :quarter]

    def scatter(src, dst, ssem, rsem):
        for j in range(1, pairs):
            pltpu.make_async_remote_copy(
                src_ref=src.at[(k + j) % pairs], dst_ref=dst.at[j - 1],
                send_sem=ssem, recv_sem=rsem,
                device_id=others[j - 1], device_id_type=MESH,
            ).start()

    xi = par * 2 + xh
    xis = [(1 - par) * 2 + xh, (1 - par) * 2 + (1 - xh), par * 2 + (1 - xh)]
    row = [dev_a, dev_b, dev_d]
    scatter(t2, ry, qs_sem.at[5], qr_sem.at[5])
    for e in range(3):
        send(t1.at[:, xis[e]], rx.at[e], qs_sem.at[2 + e], qr_sem.at[2 + e], row[e])
    for e in range(3):
        arrived(rx.at[e], qr_sem.at[2 + e])
    u1[...] = t1[:, xi] + (rx[0] + rx[1] + rx[2])
    scatter(u1, r2y, qs_sem.at[9], qr_sem.at[9])
    arrived(ry, qr_sem.at[5])
    u2[...] = t2[k] + sum(ry[j] for j in range(pairs - 1))
    for e in range(3):
        send(u2.at[xis[e]], r2x.at[e], qs_sem.at[6 + e], qr_sem.at[6 + e], row[e])
    for e in range(3):
        arrived(r2x.at[e], qr_sem.at[6 + e])
    second = u2[xi] + (r2x[0] + r2x[1] + r2x[2])
    arrived(r2y, qr_sem.at[9])
    fin[:, :quarter] = u1[k] + sum(r2y[j] for j in range(pairs - 1))
    fin[:, quarter:] = second
    send(fin, rf, qs_sem.at[10], qr_sem.at[10], dev_s)
    arrived(rf, qr_sem.at[10])
    own, other = fin[...], rf[...]
    left = jnp.where(core == 0, own, other)
    right = jnp.where(core == 0, other, own)
    rows = o_ref.shape[0]
    full = jnp.concatenate([left, right], axis=1)
    o_ref[...] = jnp.where(core == 0, full[:rows], full[rows:])

    arrived(ry, qs_sem.at[5])
    arrived(r2y, qs_sem.at[9])
    for copy in sent:
        copy.wait_send()


def shards(regions, basis_v, basis_w, couplings, coupling_cols):
    nb, slots, block, _ = couplings.shape
    basis = basis_w.shape[1]
    cb = nb // CHUNKS
    wb = nb // 4
    wh = wb // (2 * HALF_CHUNKS)
    pairs = regions // 2
    group = basis // (4 * pairs)
    quarter = basis // 4
    bf16, f32 = jnp.bfloat16, jnp.float32
    dma = pltpu.SemaphoreType.DMA
    whole = pl.BlockSpec(memory_space=pl.ANY)
    return pl.pallas_call(
        functools.partial(kernel, regions),
        out_shape=jax.ShapeDtypeStruct((group // 2, basis), f32),
        in_specs=[pl.BlockSpec(memory_space=pltpu.SMEM), whole, whole, whole],
        out_specs=pl.BlockSpec(memory_space=pltpu.VMEM),
        scratch_shapes=[
            pltpu.VMEM((nb, slots, block, block), bf16),
            pltpu.VMEM((4, 3 * nb, block, quarter), bf16),
            pltpu.VMEM((4, MIDDLE * cb, block, quarter), bf16),
            pltpu.VMEM((4, (CHUNKS - EARLY - MIDDLE) * cb, block, quarter), bf16),
            pltpu.VMEM((4, wb, block, basis), bf16),
            pltpu.VMEM((2, HALF_CHUNKS, wh, block, basis), bf16),
            pltpu.VMEM((pairs, 4, group, basis), f32),
            pltpu.VMEM((2, pairs, 4, group, quarter), f32),
            pltpu.VMEM((pairs, 4, group, quarter), f32),
            pltpu.VMEM((pairs, 4, group, quarter), f32),
            pltpu.VMEM((3, pairs, group, quarter), f32),
            pltpu.VMEM((pairs - 1, 4, group, quarter), f32),
            pltpu.VMEM((pairs, group, quarter), f32),
            pltpu.VMEM((4, group, quarter), f32),
            pltpu.VMEM((3, group, quarter), f32),
            pltpu.VMEM((pairs - 1, group, quarter), f32),
            pltpu.VMEM((group, 2 * quarter), f32),
            pltpu.VMEM((group, 2 * quarter), f32),
            pltpu.VMEM((2, 2, 2, wh, 2, block, quarter), bf16),
            dma((5,)),
            dma((5, CHUNKS)), dma((5, CHUNKS)),
            dma((6, CHUNKS)), dma((6, CHUNKS)),
            dma((1 + 6 * HALF_CHUNKS,)), dma((1 + 6 * HALF_CHUNKS,)),
            dma((8,)), dma((8,)),
            dma((11,)), dma((11,)),
        ],
        compiler_params=pltpu.CompilerParams(
            collective_id=0, has_side_effects=True, vmem_limit_bytes=67043328
        ),
        name="project",
    )(
        coupling_cols.T,
        couplings,
        basis_v.reshape(nb, block, quarter),
        basis_w.reshape(wb, block, basis),
    )


def solution(mesh):
    in_specs = (
        P("region", "col"),
        P(("region", "col"), None),
        P("region", "col", None, None),
        P("region", "col"),
    )
    out_specs = P(("region", "col"), None)
    body = functools.partial(shards, mesh.shape["region"])
    return jax.shard_map(body, mesh=mesh, in_specs=in_specs, out_specs=out_specs, check_vma=False)
```

```python
import functools

import jax
import jax.numpy as jnp
from jax import lax
from jax.experimental import pallas as pl
from jax.experimental.pallas import tpu as pltpu
from jax.sharding import PartitionSpec as P

MESH = pl.DeviceIdType.MESH
CHUNKS = 8
EARLY, MIDDLE = 5, 2
HALF_CHUNKS = 3


def kernel(
    regions, cols_ref, a_hbm, v_hbm, w_hbm, o_ref,
    a, v, y1, y2, w, wr, acc, r0, t1, t2, rx, ry, u1, u2, r2x, r2y, fin, rf,
    xs, loc, vs, vr, bs, br, ws, wrecv, xsend, xrecv, qs_sem, qr_sem,
):
    nb, slots = a.shape[0], a.shape[1]
    n, half = CHUNKS, CHUNKS // 2
    cb = nb // n
    wb = w.shape[1]
    wh = wb // (2 * HALF_CHUNKS)
    pairs = regions // 2
    basis = acc.shape[-1]
    quarter = basis // 4

    r, q = lax.axis_index("region"), lax.axis_index("col")
    par, core, xh = r % 2, q % 2, q // 2
    k = r // 2
    q2 = (q + 2) % 4
    qs = q + 1 - 2 * core
    qs2 = (qs + 2) % 4
    partner = r + 1 - 2 * par
    dev_a = (partner, q)
    dev_b = (partner, q2)
    dev_d = (r, q2)
    dev_s = (r, qs)
    dev_z = ((r + 2 - 4 * par + regions) % regions, q)
    others = [(((k + j) % pairs) * 2 + par, q) for j in range(1, pairs)]
    def near(odd):
        return 2 * nb * (1 - odd)

    get_a = pltpu.make_async_copy(a_hbm, a, loc.at[0])
    get_v = pltpu.make_async_copy(v_hbm, v.at[q, pl.ds(nb, nb)], loc.at[1])
    get_w = pltpu.make_async_copy(w_hbm, w.at[q], loc.at[2])
    get_v.start()
    get_w.start()

    barrier = pltpu.get_barrier_semaphore()
    greeted = [dev_a, dev_b, dev_d, dev_s] + others
    for dev in greeted:
        pl.semaphore_signal(barrier, inc=1, device_id=dev, device_id_type=MESH)
    pl.semaphore_wait(barrier, len(greeted))

    sent = []

    def send(src, dst, ssem, rsem, dev):
        copy = pltpu.make_async_remote_copy(
            src_ref=src, dst_ref=dst, send_sem=ssem, recv_sem=rsem,
            device_id=dev, device_id_type=MESH,
        )
        copy.start()
        sent.append(copy)

    def arrived(dst, rsem):
        pltpu.make_async_copy(dst, dst, rsem).wait()

    def place(odd, c):
        return odd * (n - 1 - c) * cb + (1 - odd) * c * cb

    def piece_here(col, odd, c):
        return v.at[col, pl.ds(nb + place(odd, c), cb)]

    def piece_near(col, odd, c):
        return v.at[col, pl.ds(near(odd) + place(1 - odd, c), cb)]

    def piece_far(col, c):
        if c < EARLY:
            return v.at[col, pl.ds(par * 2 * nb + place(1 - par, c), cb)]
        if c < EARLY + MIDDLE:
            e = c - EARLY
            return y1.at[col, pl.ds(par * e * cb + (1 - par) * (MIDDLE - 1 - e) * cb, cb)]
        e, late = c - EARLY - MIDDLE, n - EARLY - MIDDLE
        return y2.at[col, pl.ds(par * e * cb + (1 - par) * (late - 1 - e) * cb, cb)]

    for c in range(n):
        src = v_hbm.at[pl.ds(place(par, c), cb)]
        send(src, piece_near(q, 1 - par, c), vs.at[0, c], vr.at[0, c], dev_a)
        send(src, piece_near(q, 1 - par, c), vs.at[1, c], vr.at[1, c], dev_b)
    send(v_hbm, v.at[q, pl.ds(nb, nb)], bs.at[0, 0], br.at[0, 0], dev_s)
    send(w_hbm, w.at[q], ws.at[0], wrecv.at[0], dev_s)
    get_a.start()

    def to_sibling(slab, ref, c):
        send(ref, ref, bs.at[slab, c], br.at[slab, c], dev_s)

    def take_near(c):
        ref = piece_near(q, par, c)
        arrived(ref, vr.at[0, c])
        send(ref, piece_far(q, c), vs.at[3, c], vr.at[3, c], dev_z)
        if c < half:
            send(ref, piece_here(q, 1 - par, c), vs.at[2, c], vr.at[2, c], dev_b)
        to_sibling(1, ref, c)
        ref = piece_near(q2, par, c)
        arrived(ref, vr.at[1, c])
        send(ref, piece_far(q2, c), vs.at[4, c], vr.at[4, c], dev_z)
        if c >= half:
            send(ref, piece_here(q2, 1 - par, c), vs.at[2, c], vr.at[2, c], dev_a)
        to_sibling(2, ref, c)

    def take_here(c):
        ref = piece_here(q2, par, c)
        arrived(ref, vr.at[2, c])
        to_sibling(3, ref, c)

    def take_far(c):
        for e, col in ((3, q), (4, q2)):
            ref = piece_far(col, c)
            arrived(ref, vr.at[e, c])
            to_sibling(e + 1, ref, c)

    for c in range(n):
        take_near(c)

    for h in range(HALF_CHUNKS):
        send(w_hbm.at[pl.ds(h * wh, wh)], wr.at[0, h], ws.at[1 + h], wrecv.at[1 + h], dev_a)
        o = 1 + HALF_CHUNKS + h
        send(w_hbm.at[pl.ds(wb // 2 + h * wh, wh)], wr.at[1, h], ws.at[o], wrecv.at[o], dev_b)

    def relay_w(h):
        o = 1 + 2 * HALF_CHUNKS + h
        arrived(wr.at[0, h], wrecv.at[1 + h])
        send(wr.at[0, h], w.at[q, pl.ds(h * wh, wh)], ws.at[o], wrecv.at[o], dev_b)
        o = o + HALF_CHUNKS
        arrived(wr.at[1, h], wrecv.at[1 + HALF_CHUNKS + h])
        send(wr.at[1, h], w.at[q2, pl.ds(wb // 2 + h * wh, wh)], ws.at[o], wrecv.at[o], dev_a)

    for c in range(half - 1):
        take_far(c)
    for c in range(half):
        take_here(c)
        take_here(c + half)
        if c >= half - 2:
            take_far(half - 1 + c - (half - 2))

    get_v.wait()
    get_a.wait()
    arrived(v.at[qs, pl.ds(nb, nb)], br.at[0, 0])
    for c in range(n):
        arrived(piece_near(qs, par, c), br.at[1, c])
        arrived(piece_near(qs2, par, c), br.at[2, c])
        arrived(piece_here(qs2, par, c), br.at[3, c])

    def image_rows(c):
        start = place(1 - par, c)
        first = nb * r - nb

        def image_row(t, carry):
            i = start + t
            ix = [jnp.clip(cols_ref[s, i] - first, 0, 3 * nb - 1) for s in range(slots)]
            lhs = jnp.concatenate([a[i, s] for s in range(slots)], axis=1)
            rhs = jnp.concatenate(
                [jnp.concatenate([v[col, at] for col in range(4)], axis=1) for at in ix], axis=0
            )
            total = jnp.dot(lhs, rhs, preferred_element_type=jnp.float32)
            upper = total.astype(jnp.bfloat16)
            lower = (total - upper.astype(jnp.float32)).astype(jnp.bfloat16)
            for col in range(4):
                a[i, col] = upper[:, col * quarter:(col + 1) * quarter]
                a[i, 4 + col] = lower[:, col * quarter:(col + 1) * quarter]
            return carry

        lax.fori_loop(0, cb, image_row, 0)

    def all_far(first, last):
        for c in range(first, last):
            arrived(piece_far(qs, c), br.at[4, c])
            arrived(piece_far(qs2, c), br.at[5, c])

    dims = (((0,), (0,)), ((), ()))

    def image(at, count, first, cols=4):
        tiles = [a[pl.ds(at, count), first + e].reshape(count * a.shape[2], quarter) for e in range(cols)]
        return jnp.concatenate(tiles, axis=1)

    def product(pieces):
        rows = sum(count for _, count, _ in pieces) * w.shape[2]
        wv = jnp.concatenate([wv for _, _, wv in pieces], axis=0).reshape(rows, basis)
        upper, lower = [
            jnp.concatenate([image(at, count, e) for at, count, _ in pieces], axis=0)
            for e in (0, 4)
        ]
        out = lax.dot_general(wv, upper, dims, preferred_element_type=jnp.float32)
        out += lax.dot_general(wv, lower, dims, preferred_element_type=jnp.float32)
        return out.reshape(acc.shape)

    late = par * xh + (1 - par) * (1 - xh)

    def own_rows(m):
        at = (1 - par) * (n - 1 - m - late * half) * cb + par * (m + late * half) * cb
        slab = at // wb
        return at, cb, w[slab, pl.ds(at - slab * wb, cb)]

    def own_part(groups):
        return product([own_rows(m) for m in groups])

    at1 = par * (2 * nb + EARLY * cb) + (1 - par) * (n - EARLY - MIDDLE) * cb
    at2 = par * (2 * nb + (EARLY + MIDDLE) * cb)
    put1 = pltpu.make_async_copy(y1, v.at[:, pl.ds(at1, MIDDLE * cb)], loc.at[3])
    put2 = pltpu.make_async_copy(y2, v.at[:, pl.ds(at2, (n - EARLY - MIDDLE) * cb)], loc.at[4])

    def w_arrived(h):
        for part in range(2):
            o = 1 + (2 + part) * HALF_CHUNKS + h
            ref = w.at[q2, pl.ds(part * (wb // 2) + h * wh, wh)]
            arrived(ref, wrecv.at[o])
            p = o + 2 * HALF_CHUNKS
            send(ref, ref, ws.at[p], wrecv.at[p], dev_s)

    def w_forwarded(h):
        for part in range(2):
            p = 1 + (4 + part) * HALF_CHUNKS + h
            arrived(w.at[qs2, pl.ds(part * (wb // 2) + h * wh, wh)], wrecv.at[p])

    all_far(0, EARLY)
    image_rows(0)
    take_far(5)
    image_rows(1)
    relay_w(0)
    image_rows(2)
    image_rows(3)
    relay_w(1)
    image_rows(4)
    take_far(6)
    all_far(EARLY, EARLY + MIDDLE)
    put1.start()
    get_w.wait()
    arrived(w.at[qs], wrecv.at[0])
    acc[...] = own_part([0])
    put1.wait()
    image_rows(5)
    relay_w(2)
    image_rows(6)
    acc[...] += own_part([1, 2])
    take_far(7)
    all_far(EARLY + MIDDLE, n)
    put2.start()
    w_arrived(0)
    put2.wait()
    image_rows(7)

    mine = pl.multiple_of(core * (2 * quarter), 2 * quarter)
    theirs = pl.multiple_of((1 - core) * (2 * quarter), 2 * quarter)
    last = HALF_CHUNKS - 1
    lasts = [(e, part) for e in range(2) for part in range(2)]

    def last_rows(slab, part):
        return slab * wb + part * (wb // 2) + last * wh

    for e, part in lasts:
        at = last_rows(2 * (1 - xh) + e, part)
        for f in range(2):
            cut = a.at[pl.ds(at, wh), pl.ds(4 * f + 2 * (1 - core), 2)]
            g = 4 * e + 2 * part + f
            send(cut, xs.at[e, part, f], xsend.at[g], xrecv.at[g], dev_s)
    acc[...] += own_part([3])

    def both(slab, h):
        ats = [part * (wb // 2) + h * wh for part in range(2)]
        return [(slab * wb + at, wh, w[slab, at:at + wh]) for at in ats]

    for h in range(1, last):
        w_arrived(h)
    for h in range(last):
        w_forwarded(h)
        acc[...] += product(both(q2, h) + both(qs2, h))

    for e in (1, 0):
        cut = acc.at[:, :, :, pl.ds(theirs + e * quarter, quarter)]
        send(cut, r0.at[e], qs_sem.at[e], qr_sem.at[e], dev_s)
    for e, part in lasts:
        for f in range(2):
            arrived(xs.at[e, part, f], xrecv.at[4 * e + 2 * part + f])
    arrived(r0.at[1], qr_sem.at[1])
    t2[...] = acc[:, :, :, pl.ds(mine + quarter, quarter)] + r0[1]
    arrived(r0.at[0], qr_sem.at[0])
    t1[...] = acc[:, :, :, pl.ds(mine, quarter)] + r0[0]

    def last_product(slab, e):
        rows = 2 * wh * w.shape[2]
        wv = jnp.concatenate(
            [w[slab, part * (wb // 2) + last * wh:part * (wb // 2) + (last + 1) * wh] for part in range(2)],
            axis=0,
        ).reshape(rows, basis)
        wv = jnp.concatenate([wv, wv], axis=0)
        out = None
        for f in range(2):
            img = jnp.concatenate(
                [image(last_rows(slab, part), wh, 4 * f + 2 * core, 2) for part in range(2)]
                + [
                    jnp.concatenate(
                        [xs[e, part, f, :, c].reshape(rows // 2, quarter) for c in range(2)], axis=1
                    )
                    for part in range(2)
                ],
                axis=0,
            )
            term = lax.dot_general(wv, img, dims, preferred_element_type=jnp.float32)
            out = term if out is None else out + term
        return out.reshape(t1.shape[:3] + (2 * quarter,))

    w_arrived(last)
    out = last_product(q2, core)
    t2[...] += out[:, :, :, quarter:]
    t1[...] += out[:, :, :, :quarter]
    w_forwarded(last)
    out = last_product(qs2, 1 - core)
    t2[...] += out[:, :, :, quarter:]
    t1[...] += out[:, :, :, :quarter]

    def scatter(src, dst, ssem, rsem):
        for j in range(1, pairs):
            pltpu.make_async_remote_copy(
                src_ref=src.at[(k + j) % pairs], dst_ref=dst.at[j - 1],
                send_sem=ssem, recv_sem=rsem,
                device_id=others[j - 1], device_id_type=MESH,
            ).start()

    xi = par * 2 + xh
    xis = [(1 - par) * 2 + xh, (1 - par) * 2 + (1 - xh), par * 2 + (1 - xh)]
    row = [dev_a, dev_b, dev_d]
    scatter(t2, ry, qs_sem.at[5], qr_sem.at[5])
    for e in range(3):
        send(t1.at[:, xis[e]], rx.at[e], qs_sem.at[2 + e], qr_sem.at[2 + e], row[e])
    for e in range(3):
        arrived(rx.at[e], qr_sem.at[2 + e])
    u1[...] = t1[:, xi] + (rx[0] + rx[1] + rx[2])
    scatter(u1, r2y, qs_sem.at[9], qr_sem.at[9])
    arrived(ry, qr_sem.at[5])
    u2[...] = t2[k] + sum(ry[j] for j in range(pairs - 1))
    for e in range(3):
        send(u2.at[xis[e]], r2x.at[e], qs_sem.at[6 + e], qr_sem.at[6 + e], row[e])
    for e in range(3):
        arrived(r2x.at[e], qr_sem.at[6 + e])
    second = u2[xi] + (r2x[0] + r2x[1] + r2x[2])
    arrived(r2y, qr_sem.at[9])
    fin[:, :quarter] = u1[k] + sum(r2y[j] for j in range(pairs - 1))
    fin[:, quarter:] = second
    send(fin, rf, qs_sem.at[10], qr_sem.at[10], dev_s)
    arrived(rf, qr_sem.at[10])
    own, other = fin[...], rf[...]
    left = jnp.where(core == 0, own, other)
    right = jnp.where(core == 0, other, own)
    rows = o_ref.shape[0]
    full = jnp.concatenate([left, right], axis=1)
    o_ref[...] = jnp.where(core == 0, full[:rows], full[rows:])

    arrived(ry, qs_sem.at[5])
    arrived(r2y, qs_sem.at[9])
    for copy in sent:
        copy.wait_send()


def shards(regions, basis_v, basis_w, couplings, coupling_cols):
    nb, slots, block, _ = couplings.shape
    basis = basis_w.shape[1]
    cb = nb // CHUNKS
    wb = nb // 4
    wh = wb // (2 * HALF_CHUNKS)
    pairs = regions // 2
    group = basis // (4 * pairs)
    quarter = basis // 4
    bf16, f32 = jnp.bfloat16, jnp.float32
    dma = pltpu.SemaphoreType.DMA
    whole = pl.BlockSpec(memory_space=pl.ANY)
    return pl.pallas_call(
        functools.partial(kernel, regions),
        out_shape=jax.ShapeDtypeStruct((group // 2, basis), f32),
        in_specs=[pl.BlockSpec(memory_space=pltpu.SMEM), whole, whole, whole],
        out_specs=pl.BlockSpec(memory_space=pltpu.VMEM),
        scratch_shapes=[
            pltpu.VMEM((nb, slots, block, block), bf16),
            pltpu.VMEM((4, 3 * nb, block, quarter), bf16),
            pltpu.VMEM((4, MIDDLE * cb, block, quarter), bf16),
            pltpu.VMEM((4, (CHUNKS - EARLY - MIDDLE) * cb, block, quarter), bf16),
            pltpu.VMEM((4, wb, block, basis), bf16),
            pltpu.VMEM((2, HALF_CHUNKS, wh, block, basis), bf16),
            pltpu.VMEM((pairs, 4, group, basis), f32),
            pltpu.VMEM((2, pairs, 4, group, quarter), f32),
            pltpu.VMEM((pairs, 4, group, quarter), f32),
            pltpu.VMEM((pairs, 4, group, quarter), f32),
            pltpu.VMEM((3, pairs, group, quarter), f32),
            pltpu.VMEM((pairs - 1, 4, group, quarter), f32),
            pltpu.VMEM((pairs, group, quarter), f32),
            pltpu.VMEM((4, group, quarter), f32),
            pltpu.VMEM((3, group, quarter), f32),
            pltpu.VMEM((pairs - 1, group, quarter), f32),
            pltpu.VMEM((group, 2 * quarter), f32),
            pltpu.VMEM((group, 2 * quarter), f32),
            pltpu.VMEM((2, 2, 2, wh, 2, block, quarter), bf16),
            dma((5,)),
            dma((5, CHUNKS)), dma((5, CHUNKS)),
            dma((6, CHUNKS)), dma((6, CHUNKS)),
            dma((1 + 6 * HALF_CHUNKS,)), dma((1 + 6 * HALF_CHUNKS,)),
            dma((8,)), dma((8,)),
            dma((11,)), dma((11,)),
        ],
        compiler_params=pltpu.CompilerParams(
            collective_id=0, has_side_effects=True, vmem_limit_bytes=67043328
        ),
        name="project",
    )(
        coupling_cols.T,
        couplings,
        basis_v.reshape(nb, block, quarter),
        basis_w.reshape(wb, block, basis),
    )


def solution(mesh):
    in_specs = (
        P("region", "col"),
        P(("region", "col"), None),
        P("region", "col", None, None),
        P("region", "col"),
    )
    out_specs = P(("region", "col"), None)
    body = functools.partial(shards, mesh.shape["region"])
    return jax.shard_map(body, mesh=mesh, in_specs=in_specs, out_specs=out_specs, check_vma=False)
```
